768 devices in a mesh: space: 192 (over y, z, core), traj: 4 (over x).
Axes of the slice: x: 4, y: 8, z: 12, core: 2. Of those that a mesh axis runs over, the one named last changes fastest.
Arguments:
- field: float32 [4, 39, 1536, 256], P('traj', None, 'space'), may hold values from -6 to 6
- solid: int32 [4, 1536, 256], P('traj', 'space'), may hold values 0 or 1
- cotangent: float32 [4, 39, 1536, 256], P('traj', None, 'space'), may hold values from -6 to 6
- w_in: bfloat16 [20, 512], replicated, may hold values from -1.25 to 1.25
- b_in: float32 [512], replicated, may hold values from -3 to 3
- w_out: bfloat16 [512, 39], replicated, may hold values from -0.25 to 0.25
- b_out: float32 [39], replicated, may hold values from -3 to 3
Outputs:
- d_field: float32 [4, 39, 1536, 256], P('traj', None, 'space')
- g_w_in: float32 [20, 512], replicated
- g_b_in: float32 [512], replicated
- g_w_out: float32 [512, 39], replicated
- g_b_out: float32 [39], replicated
The draws below stay inside these ranges and needn't reach their ends.
All inputs are finite; a program needn't handle non-finite values. No bound on the sum of `solid` on one device may be relied on, other than what follows from the above.
Results may differ from the reference program's by a relative error of at most 0.0089.
Values sent between devices are 32-bit elements; how exact they have to be, the bound alone decides.
A program may use at most 32 MiB of HBM per device.

```python
import math
import jax
import jax.numpy as jnp
from jax import lax

Q = 39
MOM = 20
HID = 512
STEPS = 3
NX = 16
NY = 16
CZ = 8
PLANE = 256
NZ = 1536
TRAJ = 4


def with_ends(drawn, rng, least, top_value):
    longest = drawn.shape.index(max(drawn.shape))
    spots = []
    for shift in (0, 1):
        where = [jax.random.randint(jax.random.fold_in(rng, axis), (), 0, length) for axis, length in enumerate(drawn.shape)]
        where[longest] = (where[longest] + shift) % drawn.shape[longest]
        spots.append(tuple(where))
    return drawn.at[spots[0]].set(least).at[spots[1]].set(top_value)


def levels(rng, dims, split, low, high):
    factor_of = 1.0
    for position, parts in split:
        heights = jax.random.uniform(jax.random.fold_in(jax.random.fold_in(rng, 6), position), (parts,), jnp.float32, low / len(split), high / len(split))
        factor_of = factor_of * jnp.repeat(jnp.exp(heights), dims[position] // parts).reshape((-1,) + (1,) * (len(dims) - 1 - position))
    return factor_of


def noise(key, shape, deviation, most, shards=(), kind=jnp.bfloat16):
    array = jax.random.normal(key, shape, jnp.float32) * deviation
    if len(shards) > 0:
        array = levels(key, shape, shards, -0.22, 0.18) * array
    return jnp.clip(array, min=-most, max=most).astype(kind)


def setup_inputs(seed: int = 0) -> dict:
    seeds = jax.random.split(jax.random.key(seed), 8)
    field = noise(seeds[0], (TRAJ, Q, NZ, PLANE), 1.0, 6.0, ((0, 4), (2, 192)), jnp.float32)
    solid = with_ends((jax.random.randint(seeds[1], (TRAJ, NZ, PLANE), 0, 8) < 1).astype(jnp.int32), jax.random.fold_in(seeds[1], 1), 0, 1)
    cotangent = noise(seeds[2], (TRAJ, Q, NZ, PLANE), 1.0, 6.0, ((0, 4), (2, 192)), jnp.float32)
    w_in = noise(seeds[3], (MOM, HID), MOM ** -0.5, 1.25)
    b_in = noise(seeds[4], (HID,), 0.5, 3.0, (), jnp.float32)
    w_out = noise(seeds[5], (HID, Q), HID ** -0.5, 0.25)
    b_out = noise(seeds[6], (Q,), 0.5, 3.0, (), jnp.float32)
    return {"field": field, "solid": solid, "cotangent": cotangent, "w_in": w_in, "b_in": b_in, "w_out": w_out, "b_out": b_out}


def velocity_table():
    rows = [(0, 0, 0)]
    for axis_one in range(3):
        for sign in (1, -1):
            entry = [0, 0, 0]
            entry[axis_one] = sign
            rows.append(tuple(entry))
    for along_x in (1, -1):
        for along_y in (1, -1):
            for along_z in (1, -1):
                rows.append((along_x, along_y, along_z))
    for axis_one in range(3):
        for sign in (1, -1):
            entry = [0, 0, 0]
            entry[axis_one] = 2 * sign
            rows.append(tuple(entry))
    for first, second in ((0, 1), (0, 2), (1, 2)):
        for sign_one in (2, -2):
            for sign_two in (2, -2):
                entry = [0, 0, 0]
                entry[first] = sign_one
                entry[second] = sign_two
                rows.append(tuple(entry))
    for axis_one in range(3):
        for sign in (1, -1):
            entry = [0, 0, 0]
            entry[axis_one] = 3 * sign
            rows.append(tuple(entry))
    return rows

def opposite_index(velocity):
    result = []
    for row in velocity:
        flipped = (-row[0], -row[1], -row[2])
        result.append(velocity.index(flipped))
    return result

def hermite_table(velocity):
    sound = 2.0 / 3.0
    ident = [[1.0 if a == b else 0.0 for b in range(3)] for a in range(3)]
    speed = [[float(v) for v in row] for row in velocity]
    rows = [[1.0 for row in speed]]
    for first in range(3):
        rows.append([row[first] for row in speed])
    for first in range(3):
        for second in range(first, 3):
            rows.append([row[first] * row[second] - sound * ident[first][second] for row in speed])
    for first in range(3):
        for second in range(first, 3):
            for third in range(second, 3):
                rows.append([row[first] * row[second] * row[third] - sound * (row[first] * ident[second][third] + row[second] * ident[first][third] + row[third] * ident[first][second]) for row in speed])
    normed = []
    for values in rows:
        length = math.sqrt(sum((v * v for v in values)))
        normed.append([v / length for v in values])
    return jnp.asarray(normed, jnp.float32)

def collide_block(block, weights, hermite):
    w_in, b_in, w_out, b_out = weights
    moments = jnp.dot(hermite, block, precision=lax.Precision.HIGHEST, preferred_element_type=jnp.float32)
    rounded = moments.astype(jnp.bfloat16)
    hidden = jnp.tanh(jnp.dot(w_in.T, rounded, preferred_element_type=jnp.float32) + b_in[:, None]).astype(jnp.bfloat16)
    change = jnp.dot(w_out.T, hidden, preferred_element_type=jnp.float32) + b_out[:, None]
    return (block + change, rounded, hidden)

def adjoint_block(block, incoming, weights, hermite):
    w_in, b_in, w_out, b_out = weights
    unused, rounded, hidden = collide_block(block, weights, hermite)
    grad_rounded = incoming.astype(jnp.bfloat16)
    d_hidden = jnp.dot(w_out, grad_rounded, preferred_element_type=jnp.float32)
    hidden_wide = hidden.astype(jnp.float32)
    d_act = (d_hidden * (1.0 - hidden_wide * hidden_wide)).astype(jnp.bfloat16)
    d_moments = jnp.dot(w_in, d_act, preferred_element_type=jnp.float32)
    d_block = incoming + jnp.dot(hermite.T, d_moments, precision=lax.Precision.HIGHEST, preferred_element_type=jnp.float32)
    grads = (jnp.dot(rounded, d_act.T, preferred_element_type=jnp.float32), lax.optimization_barrier(jnp.sum(d_act.astype(jnp.float32), axis=1)), jnp.dot(hidden, grad_rounded.T, preferred_element_type=jnp.float32), lax.optimization_barrier(jnp.sum(incoming, axis=1)))
    return (d_block, grads)

def split_blocks(values):
    count = values.shape[1] // CZ
    return jnp.moveaxis(values.reshape(values.shape[0], count, CZ * values.shape[2]), 1, 0)

def join_blocks(blocks, shape):
    return jnp.moveaxis(blocks, 0, 1).reshape(shape)

def collide_field(state, weights, hermite):
    blocks = lax.map(lambda block: collide_block(block, weights, hermite)[0], split_blocks(state))
    return join_blocks(blocks, state.shape)

def adjoint_field(state, incoming, weights, hermite):
    zeros = tuple((jnp.zeros(w.shape, jnp.float32) for w in weights))

    def advance(totals, pair):
        d_block, grads = adjoint_block(pair[0], pair[1], weights, hermite)
        return (tuple((a + b for a, b in zip(totals, grads))), d_block)
    totals, blocks = lax.scan(advance, zeros, (split_blocks(state), split_blocks(incoming)))
    return (join_blocks(blocks, state.shape), totals)

def roll_plane(rows, along_x, along_y):
    depth = rows.shape[0]
    grid = rows.reshape(depth, NX, NY)
    return jnp.roll(grid, (along_x, along_y), (1, 2)).reshape(depth, NX * NY)

def stream_whole(state, velocity, sign):
    moved = []
    for index in range(len(velocity)):
        along_x = sign * velocity[index][0]
        along_y = sign * velocity[index][1]
        along_z = sign * velocity[index][2]
        part = jnp.roll(state[index], along_z, 0)
        moved.append(roll_plane(part, along_x, along_y))
    return jnp.stack(moved)

def reference(field, solid, cotangent, w_in, b_in, w_out, b_out):
    velocity = velocity_table()
    opposite = opposite_index(velocity)
    hermite = hermite_table(velocity)
    weights = (w_in, b_in, w_out, b_out)
    totals = tuple((jnp.zeros(w.shape, jnp.float32) for w in weights))
    results = []
    for trajectory in range(TRAJ):
        wall = solid[trajectory].astype(jnp.float32)[None]
        fluid = 1.0 - wall
        current = field[trajectory]
        states = []
        for step in range(STEPS):
            states.append(current)
            post = collide_field(current, weights, hermite)
            current = fluid * stream_whole(post, velocity, 1) + wall * post[jnp.asarray(opposite, jnp.int32)]
        back = cotangent[trajectory]
        for step in range(STEPS - 1, -1, -1):
            incoming = stream_whole(fluid * back, velocity, -1) + (wall * back)[jnp.asarray(opposite, jnp.int32)]
            back, grads = adjoint_field(states[step], incoming, weights, hermite)
            totals = tuple((a + b for a, b in zip(totals, grads)))
        results.append(back)
    scale = 1.0 / math.sqrt(float(TRAJ * NZ * PLANE * STEPS))
    return (jnp.stack(results), totals[0] * scale, totals[1] * scale, totals[2] * scale, totals[3] * scale)
```

```python
import math

import jax
import jax.numpy as jnp
import numpy as np
from jax import lax
from jax.experimental import pallas as pl
from jax.experimental.pallas import tpu as pltpu
from jax.sharding import PartitionSpec as P

STEPS = 3
Q = 39
MOM = 20
HID = 512
CZ = 8
PLANE = 256
ROWS = 40
CELLS = CZ * PLANE
MESH = pl.DeviceIdType.MESH
F32 = jnp.float32
BF16 = jnp.bfloat16
NT = (((1,), (1,)), ((), ()))


def velocity_table():
    rows = [(0, 0, 0)]
    for axis_one in range(3):
        for sign in (1, -1):
            entry = [0, 0, 0]
            entry[axis_one] = sign
            rows.append(tuple(entry))
    for along_x in (1, -1):
        for along_y in (1, -1):
            for along_z in (1, -1):
                rows.append((along_x, along_y, along_z))
    for axis_one in range(3):
        for sign in (1, -1):
            entry = [0, 0, 0]
            entry[axis_one] = 2 * sign
            rows.append(tuple(entry))
    for first, second in ((0, 1), (0, 2), (1, 2)):
        for sign_one in (2, -2):
            for sign_two in (2, -2):
                entry = [0, 0, 0]
                entry[first] = sign_one
                entry[second] = sign_two
                rows.append(tuple(entry))
    for axis_one in range(3):
        for sign in (1, -1):
            entry = [0, 0, 0]
            entry[axis_one] = 3 * sign
            rows.append(tuple(entry))
    return rows


def hermite_table(velocity):
    sound = 2.0 / 3.0
    e = np.asarray(velocity, np.float64)
    ident = np.eye(3)
    rows = [np.ones(len(velocity))]
    for a in range(3):
        rows.append(e[:, a])
    for a in range(3):
        for b in range(a, 3):
            rows.append(e[:, a] * e[:, b] - sound * ident[a, b])
    for a in range(3):
        for b in range(a, 3):
            for c in range(b, 3):
                rows.append(
                    e[:, a] * e[:, b] * e[:, c]
                    - sound * (e[:, a] * ident[b, c] + e[:, b] * ident[a, c] + e[:, c] * ident[a, b])
                )
    return np.stack([r / np.sqrt((r * r).sum()) for r in rows]).astype(np.float32)


def row_order(velocity):
    up = [(0, 0, 3), (0, 0, 2), (2, 0, 2), (-2, 0, 2), (0, 2, 2), (0, -2, 2), (0, 0, 1), (1, 1, 1)]
    mixed = [(1, -1, 1), (-1, 1, 1), (-1, -1, 1), (1, 0, 0)]
    level = [(0, 1, 0), (2, 0, 0), (0, 2, 0), (2, 2, 0), (2, -2, 0), (3, 0, 0), (0, 3, 0)]
    neg = lambda group: [tuple(-v for v in e) for e in group]
    order = up + mixed + neg(mixed) + neg(up) + level + [(0, 0, 0)] + neg(level)
    assert sorted(order) == sorted(velocity)
    return order


def tables():
    velocity = velocity_table()
    order = row_order(velocity)
    where = [velocity.index(e) for e in order]
    herm = hermite_table(velocity)[:, where]
    herm = np.concatenate([herm, np.zeros((MOM, 1), np.float32)], axis=1)
    bf = lambda a: np.asarray(jnp.asarray(a).astype(BF16).astype(F32))
    hi = bf(herm)
    mid = bf(herm - hi)
    low = bf(herm - hi - mid)
    thick = np.concatenate([hi, mid, low, np.zeros((4, ROWS), np.float32)])
    spread = np.zeros((64, 128), np.float32)
    for part in range(3):
        spread[:, part * ROWS : (part + 1) * ROWS] = thick
    for part in range(3):
        spread[60 + part, 120 + part] = 1.0
    final = np.zeros((24, 128), np.float32)
    final[:MOM, :ROWS] = herm
    final[:MOM, ROWS : 2 * ROWS] = herm
    final[MOM, 120] = 1.0
    pick = np.zeros((48, 128), np.float32)
    for row, q in enumerate(where):
        pick[row, q] = 1.0
    floats = np.zeros((320, 128), np.float32)
    floats[0:64] = spread
    floats[64:88] = final
    floats[88:136] = pick
    floats[136:184, :48] = pick.T[:48, :48]
    floats[184:224, :64] = thick.T
    ints = np.zeros((4, ROWS, 128), np.int32)
    for row, e in enumerate(order):
        for back, sign in ((0, 1), (1, -1)):
            for lane in range(128):
                x, y = lane // 16, lane % 16
                source = ((x - sign * e[0]) % 16) * 16 + (y - sign * e[1]) % 16
                ints[2 * back, row, lane] = source % 128
                ints[2 * back + 1, row, lane] = source // 128
    ints[0, 39], ints[2, 39] = np.arange(128), np.arange(128)
    return where, floats, ints


WHERE, FLOATS, INTS = tables()


def kernel(
    grid, scale, field, solid, cotangent, w_in, b_in, w_out, b_out, floats, ints, d_field, sums,
    pads, start, back_in, state, bounce, walls, xs, hid, dact, gbs, w_stack, w_trans, wo, wo_trans, bias, acc_in, acc_out,
    acc_b, parts, from_core, from_y, from_x, from_z, merged, final,
    halo_send, halo_recv, core_send, core_recv, y_send, y_recv, x_send, x_recv, z_send, z_recv, e_send, e_recv,
):
    ny, nz, nx = grid
    me_s, me_x = lax.axis_index("space"), lax.axis_index("traj")
    core = lax.rem(me_s, 2)
    me_z = lax.rem(me_s // 2, nz)
    me_y = me_s // (2 * nz)
    n_space = ny * nz * 2
    up = (lax.rem(me_s + 1, n_space), me_x)
    down = (lax.rem(me_s + n_space - 1, n_space), me_x)
    place = lambda y, z, c: (y * nz + z) * 2 + c
    partner = (place(me_y, me_z, 1 - core), me_x)
    at_y = lambda k: (place(lax.rem(me_y + k, ny), me_z, core), me_x)
    at_z = lambda k: (place(me_y, lax.rem(me_z + k, nz), core), me_x)
    at_x = lambda k: (me_s, lax.rem(me_x + k, nx))
    peers = [up, down] + [at_y(k) for k in range(1, ny)] + [at_x(k) for k in range(1, nx)] + [at_z(k) for k in range(1, nz)]

    barrier = pltpu.get_barrier_semaphore()
    for peer in peers:
        pl.semaphore_signal(barrier, inc=1, device_id=peer, device_id_type=MESH)

    w = w_in[...].astype(F32)
    b = b_in[...]
    b_hi = b.astype(BF16).astype(F32)
    b_mid = (b - b_hi).astype(BF16).astype(F32)
    b_low = b - b_hi - b_mid
    stack = jnp.concatenate([w, w, w, b_hi, b_mid, b_low, jnp.zeros((1, HID), F32)], axis=0)
    spread = floats[0:64, :].astype(BF16)
    full = jnp.dot(stack.T.astype(BF16), spread, preferred_element_type=F32)
    column = lax.broadcasted_iota(jnp.int32, (HID, 128), 1)
    low_part = full - full.astype(BF16).astype(F32)
    w_stack[...] = jnp.where((column >= 2 * ROWS) & (column < 3 * ROWS), low_part, full).astype(BF16)
    thick_t = floats[184:224, 0:64].astype(BF16)
    w_trans[...] = jnp.dot(thick_t, stack.astype(BF16), preferred_element_type=F32).astype(BF16)
    pick = floats[88:136, 0:Q].astype(BF16)
    by_row = jnp.dot(pick, w_out[...], preferred_element_type=F32)
    wo[...] = by_row.T.astype(BF16)
    wo_trans[...] = by_row[:ROWS].astype(BF16)
    bo = lax.dot_general(
        floats[88:136, 0:Q], jnp.broadcast_to(b_out[...], (8, Q)), NT, precision=lax.Precision.HIGHEST, preferred_element_type=F32
    )
    bias[...] = jnp.broadcast_to(bo[:ROWS, 0:1], (ROWS, PLANE))
    acc_b[...] = jnp.zeros((ROWS, PLANE), F32)

    zeros = jnp.zeros((CZ, 128), F32)
    for half in range(2):
        lanes = slice(128 * half, 128 * half + 128)
        for row in range(ROWS):
            if row < Q:
                start[half, pl.ds(row, CZ, stride=ROWS), :] = field[0, WHERE[row], :, lanes]
                back_in[half, pl.ds(row, CZ, stride=ROWS), :] = cotangent[0, WHERE[row], :, lanes]
            else:
                start[half, pl.ds(row, CZ, stride=ROWS), :] = zeros
                back_in[half, pl.ds(row, CZ, stride=ROWS), :] = zeros
    for z in range(CZ):
        walls[z] = jnp.broadcast_to(solid[0, z : z + 1, :], (8, PLANE))

    row8 = lax.broadcasted_iota(jnp.int32, (8, PLANE), 0)

    def wall_of(z):
        return walls[z] > 0

    def opposite(v):
        last = row8 == 7
        return jnp.concatenate(
            [
                v[16:24],
                jnp.concatenate([v[12:16], v[8:12]], axis=0),
                v[0:8],
                jnp.where(last, v[24:32], v[32:40]),
                jnp.where(last, v[32:40], v[24:32]),
            ],
            axis=0,
        )

    def select(wall, a, b):
        return jnp.concatenate([jnp.where(wall, a[8 * i : 8 * i + 8], b[8 * i : 8 * i + 8]) for i in range(5)], axis=0)

    def streamed(pad, z, sign):
        here = z + 3
        plane = lambda by, rows: pad[here - sign * by, rows, :]
        a, m, o, r = slice(0, 8), slice(8, 16), slice(16, 24), slice(24, 40)
        top = jnp.where(row8 == 0, plane(3, a), jnp.where(row8 < 6, plane(2, a), plane(1, a)))
        mix = jnp.where(row8 < 3, plane(1, m), jnp.where((row8 > 3) & (row8 < 7), plane(-1, m), plane(0, m)))
        low = jnp.where(row8 == 0, plane(-3, o), jnp.where(row8 < 6, plane(-2, o), plane(-1, o)))
        v = jnp.concatenate([top, mix, low, plane(0, r)], axis=0)
        which = 0 if sign == 1 else 2
        index, far = ints[which], ints[which + 1] > 0
        left = jnp.take_along_axis(v[:, 0:128], index, axis=1, mode="promise_in_bounds")
        right = jnp.take_along_axis(v[:, 128:256], index, axis=1, mode="promise_in_bounds")
        return jnp.concatenate([jnp.where(far, right, left), jnp.where(far, left, right)], axis=1)

    def cells_of(z):
        return pl.ds(pl.multiple_of(z * PLANE, PLANE), PLANE)

    def loaded(ref, z):
        rows = pl.ds(pl.multiple_of(z * ROWS, 8), ROWS)
        return jnp.concatenate([ref[0, rows, :], ref[1, rows, :]], axis=1)

    ones = jnp.ones((8, PLANE), F32)

    def hidden(t, z, v):
        v_hi = v.astype(BF16).astype(F32)
        v_low = v - v_hi
        x = jnp.concatenate([v_hi, v_low, v_hi, ones], axis=0).astype(BF16)
        xs[t, :, cells_of(z)] = x
        for c in range(2):
            rows = slice(256 * c, 256 * c + 256)
            act = jnp.dot(w_stack[rows, :], x, preferred_element_type=F32)
            hid[t, rows, cells_of(z)] = jnp.tanh(act).astype(BF16)

    def forward(t, z):
        if t == 0:
            v = loaded(start, z)
        else:
            pad = pads.at[t]
            v = select(wall_of(z), opposite(pad[z + 3]), streamed(pad, z, 1))
        hidden(t, z, v)
        if t < 2:
            change = jnp.dot(wo_trans[...], hid[t, :, cells_of(z)], preferred_element_type=F32)
            pads[t + 1, z + 3] = v + change + bias[...]

    def outgoing(z, g, slot):
        wall = wall_of(z)
        nothing = jnp.zeros((ROWS, PLANE), F32)
        bounce[z] = select(wall, opposite(g), nothing)
        pads[slot, z + 3] = select(wall, nothing, g)

    def backward(t, z):
        slot = (4, 3, 0)[t]
        g_post = streamed(pads.at[slot], z, -1) + bounce[z]
        acc_b[...] += g_post
        gb = jnp.concatenate([g_post, jnp.zeros((8, PLANE), F32)], axis=0).astype(BF16)
        gbs[:, cells_of(z)] = gb
        for c in range(2):
            rows = slice(256 * c, 256 * c + 256)
            dh = jnp.dot(wo[rows, :], gb, preferred_element_type=F32)
            h = hid[t, rows, cells_of(z)].astype(F32)
            dact[rows, cells_of(z)] = (dh * (1.0 - h * h)).astype(BF16)
        state[z] = g_post + jnp.dot(w_trans[...], dact[:, cells_of(z)], preferred_element_type=F32)

    def grads(t):
        g_in = lax.dot_general(dact[...], xs[t], NT, preferred_element_type=F32)
        g_out = lax.dot_general(hid[t], gbs[...], NT, preferred_element_type=F32)
        if t == 2:
            acc_in[...] = g_in
            acc_out[...] = g_out
        else:
            acc_in[...] += g_in
            acc_out[...] += g_out

    def halo(slot, sign):
        first, second = (up, down) if sign == 1 else (down, up)
        pad = pads.at[slot]
        if sign == 1:
            moves = [
                (pad.at[10, 0:16], pad.at[2, 0:16], up),
                (pad.at[8:10, 0:8], pad.at[0:2, 0:8], up),
                (pad.at[3, 8:24], pad.at[11, 8:24], down),
                (pad.at[4:6, 16:24], pad.at[12:14, 16:24], down),
            ]
        else:
            moves = [
                (pad.at[3, 0:16], pad.at[11, 0:16], down),
                (pad.at[4:6, 0:8], pad.at[12:14, 0:8], down),
                (pad.at[10, 8:24], pad.at[2, 8:24], up),
                (pad.at[8:10, 16:24], pad.at[0:2, 16:24], up),
            ]
        return [
            pltpu.make_async_remote_copy(
                src_ref=src, dst_ref=dst, send_sem=halo_send.at[slot, i], recv_sem=halo_recv.at[slot, i],
                device_id=to, device_id_type=MESH,
            )
            for i, (src, dst, to) in enumerate(moves)
        ]

    def begin(copies):
        for copy in copies:
            copy.start()

    def end(copies):
        for copy in copies:
            copy.wait_recv()

    def every(body):
        def two(i, carry):
            body(i)
            body(i + 4)
            return carry
        lax.fori_loop(0, 4, two, 0)

    def middle(body):
        body(3)
        body(4)

    def outer(body):
        def two(i, carry):
            body(i)
            body(i + 5)
            return carry
        lax.fori_loop(0, 3, two, 0)

    every(lambda z: forward(0, z))
    pl.semaphore_wait(barrier, len(peers))
    copy_1 = halo(1, 1)
    begin(copy_1)
    every(lambda z: outgoing(z, loaded(back_in, z), 0))
    copy_0 = halo(0, -1)
    begin(copy_0)
    middle(lambda z: forward(1, z))
    end(copy_1)
    outer(lambda z: forward(1, z))
    copy_2 = halo(2, 1)
    begin(copy_2)
    middle(lambda z: forward(2, z))
    end(copy_2)
    outer(lambda z: forward(2, z))
    end(copy_0)
    every(lambda z: backward(2, z))
    every(lambda z: outgoing(z, state[z], 3))
    copy_3 = halo(3, -1)
    begin(copy_3)
    grads(2)
    middle(lambda z: backward(1, z))
    end(copy_3)
    outer(lambda z: backward(1, z))
    every(lambda z: outgoing(z, state[z], 4))
    copy_4 = halo(4, -1)
    begin(copy_4)
    grads(1)
    middle(lambda z: backward(0, z))
    end(copy_4)
    outer(lambda z: backward(0, z))
    grads(0)

    exact = lax.Precision.HIGHEST
    upper = lax.dot_general(floats[64:88, :], acc_in[...], NT, precision=exact, preferred_element_type=F32)
    lower = lax.dot_general(floats[136:176, 0:48], acc_out[...], NT, precision=exact, preferred_element_type=F32)
    by_q = jnp.dot(floats[136:184, 0:ROWS], acc_b[...], precision=exact, preferred_element_type=F32)
    ordered = jnp.concatenate([by_q, jnp.zeros((80, PLANE), F32)], axis=0)
    line = lax.dot_general(jnp.ones((8, PLANE), F32), ordered, NT, precision=exact, preferred_element_type=F32)
    line = jnp.concatenate([line, jnp.zeros((8, HID - 128), F32)], axis=1)
    block = jnp.concatenate([upper, lower], axis=0)
    tail = jnp.where(lax.broadcasted_iota(jnp.int32, (8, HID), 0) == 7, line, block[56:64])
    block = jnp.concatenate([block[:56], tail], axis=0)
    for i in range(8):
        for j in range(4):
            parts[4 * i + j] = block[8 * i : 8 * i + 8, 128 * j : 128 * j + 128]

    def remote(src, dst, send, recv, to):
        return pltpu.make_async_remote_copy(
            src_ref=src, dst_ref=dst, send_sem=send, recv_sem=recv, device_id=to, device_id_type=MESH
        )

    mine = pl.multiple_of(core * 16, 16)
    other = pl.multiple_of((1 - core) * 16, 16)
    swap = remote(parts.at[pl.ds(other, 16)], from_core, core_send.at[0], core_recv.at[0], partner)
    swap.start()

    for half in range(2):
        for z in range(CZ):
            start[half, ROWS * z : ROWS * z + ROWS, :] = state[z, :, 128 * half : 128 * half + 128]
    for half in range(2):
        for row in range(Q):
            d_field[0, WHERE[row], :, 128 * half : 128 * half + 128] = start[half, pl.ds(row, CZ, stride=ROWS), :]

    swap.wait_recv()
    merged[...] = parts[pl.ds(mine, 16)] + from_core[...]
    per = 16 // ny
    scatter = []
    for k in range(ny - 1, 0, -1):
        piece = lax.rem(me_y + k, ny) * per
        scatter.append(remote(merged.at[pl.ds(piece, per)], from_y.at[k - 1], y_send.at[k - 1], y_recv.at[k - 1], at_y(k)))
    begin(scatter)
    end(scatter)
    total = merged[pl.ds(me_y * per, per)]
    for k in range(ny - 1):
        total = total + from_y[k]

    from_x[me_x] = total
    across = [
        remote(from_x.at[me_x], from_x.at[me_x], x_send.at[k - 1], x_recv.at[k - 1], at_x(k)) for k in range(1, nx)
    ]
    begin(across)
    end(across)
    total = from_x[0]
    for k in range(1, nx):
        total = total + from_x[k]

    from_z[me_z] = total
    far_first = sorted(range(1, nz), key=lambda k: -min(k, nz - k))
    along = [
        remote(from_z.at[me_z], from_z.at[me_z], z_send.at[k - 1], z_recv.at[k - 1], at_z(k)) for k in far_first
    ]
    begin(along)
    end(along)
    total = from_z[0]
    for k in range(1, nz):
        total = total + from_z[k]

    own = pl.ds(core * 16 + me_y * per, per)
    final[own] = total * scale
    spread_out = [
        remote(final.at[own], final.at[own], e_send.at[k - 1], e_recv.at[k - 1], at_y(k)) for k in range(ny - 1, 0, -1)
    ]
    begin(spread_out)
    end(spread_out)
    give = remote(final.at[pl.ds(mine, 16)], final.at[pl.ds(mine, 16)], core_send.at[1], core_recv.at[1], partner)
    give.start()
    give.wait_recv()
    for i in range(8):
        for j in range(4):
            sums[8 * i : 8 * i + 8, 128 * j : 128 * j + 128] = final[4 * i + j]

    for copies in (copy_0, copy_1, copy_2, copy_3, copy_4, [swap], scatter, across, along, spread_out, [give]):
        for copy in copies:
            copy.wait_send()


def solution(mesh):
    n_space, nx = mesh.shape["space"], mesh.shape["traj"]
    ny = 8 if n_space % 16 == 0 else 2
    nz = n_space // (2 * ny)
    scale = 1.0 / math.sqrt(float(n_space * nx * CELLS * STEPS))
    per = 16 // ny
    vmem = pl.BlockSpec(memory_space=pltpu.VMEM)
    dma = pltpu.SemaphoreType.DMA

    def per_device(field, solid, cotangent, w_in, b_in, w_out, b_out):
        def body(*refs):
            kernel((ny, nz, nx), scale, *refs)

        d_field, sums = pl.pallas_call(
            body,
            out_shape=(jax.ShapeDtypeStruct(field.shape, F32), jax.ShapeDtypeStruct((64, HID), F32)),
            in_specs=[vmem] * 9,
            out_specs=(vmem, vmem),
            scratch_shapes=[
                pltpu.VMEM((5, CZ + 6, ROWS, PLANE), F32),
                pltpu.VMEM((2, CZ * ROWS, 128), F32),
                pltpu.VMEM((2, CZ * ROWS, 128), F32),
                pltpu.VMEM((CZ, ROWS, PLANE), F32),
                pltpu.VMEM((CZ, ROWS, PLANE), F32),
                pltpu.VMEM((CZ, 8, PLANE), jnp.int32),
                pltpu.VMEM((STEPS, 128, CELLS), BF16),
                pltpu.VMEM((STEPS, HID, CELLS), BF16),
                pltpu.VMEM((HID, CELLS), BF16),
                pltpu.VMEM((48, CELLS), BF16),
                pltpu.VMEM((HID, 128), BF16),
                pltpu.VMEM((ROWS, HID), BF16),
                pltpu.VMEM((HID, 48), BF16),
                pltpu.VMEM((ROWS, HID), BF16),
                pltpu.VMEM((ROWS, PLANE), F32),
                pltpu.VMEM((HID, 128), F32),
                pltpu.VMEM((HID, 48), F32),
                pltpu.VMEM((ROWS, PLANE), F32),
                pltpu.VMEM((32, 8, 128), F32),
                pltpu.VMEM((16, 8, 128), F32),
                pltpu.VMEM((ny - 1, per, 8, 128), F32),
                pltpu.VMEM((nx, per, 8, 128), F32),
                pltpu.VMEM((nz, per, 8, 128), F32),
                pltpu.VMEM((16, 8, 128), F32),
                pltpu.VMEM((32, 8, 128), F32),
                dma((5, 4)), dma((5, 4)), dma((2,)), dma((2,)), dma((ny - 1,)), dma((ny - 1,)),
                dma((max(nx - 1, 1),)), dma((max(nx - 1, 1),)), dma((nz - 1,)), dma((nz - 1,)), dma((ny - 1,)), dma((ny - 1,)),
            ],
            compiler_params=pltpu.CompilerParams(collective_id=0, has_side_effects=True, vmem_limit_bytes=48 << 20),
            name="adjoint",
        )(field, solid, cotangent, w_in, b_in.reshape(1, HID), w_out.T, b_out.reshape(1, Q), jnp.asarray(FLOATS), jnp.asarray(INTS))
        return d_field, sums[:MOM], sums[MOM], sums[24:63].T, sums[63, :Q]

    return jax.shard_map(
        per_device,
        mesh=mesh,
        in_specs=(P("traj", None, "space", None), P("traj", "space", None), P("traj", None, "space", None), P(), P(), P(), P()),
        out_specs=(P("traj", None, "space", None), P(), P(), P(), P()),
        check_vma=False,
    )
```

```python
import math

import jax
import jax.numpy as jnp
import numpy as np
from jax import lax
from jax.experimental import pallas as pl
from jax.experimental.pallas import tpu as pltpu
from jax.sharding import PartitionSpec as P

STEPS = 3
Q = 39
MOM = 20
HID = 512
CZ = 8
PLANE = 256
ROWS = 40
CELLS = CZ * PLANE
MESH = pl.DeviceIdType.MESH
F32 = jnp.float32
BF16 = jnp.bfloat16
NT = (((1,), (1,)), ((), ()))


def velocity_table():
    rows = [(0, 0, 0)]
    for axis_one in range(3):
        for sign in (1, -1):
            entry = [0, 0, 0]
            entry[axis_one] = sign
            rows.append(tuple(entry))
    for along_x in (1, -1):
        for along_y in (1, -1):
            for along_z in (1, -1):
                rows.append((along_x, along_y, along_z))
    for axis_one in range(3):
        for sign in (1, -1):
            entry = [0, 0, 0]
            entry[axis_one] = 2 * sign
            rows.append(tuple(entry))
    for first, second in ((0, 1), (0, 2), (1, 2)):
        for sign_one in (2, -2):
            for sign_two in (2, -2):
                entry = [0, 0, 0]
                entry[first] = sign_one
                entry[second] = sign_two
                rows.append(tuple(entry))
    for axis_one in range(3):
        for sign in (1, -1):
            entry = [0, 0, 0]
            entry[axis_one] = 3 * sign
            rows.append(tuple(entry))
    return rows


def hermite_table(velocity):
    sound = 2.0 / 3.0
    e = np.asarray(velocity, np.float64)
    ident = np.eye(3)
    rows = [np.ones(len(velocity))]
    for a in range(3):
        rows.append(e[:, a])
    for a in range(3):
        for b in range(a, 3):
            rows.append(e[:, a] * e[:, b] - sound * ident[a, b])
    for a in range(3):
        for b in range(a, 3):
            for c in range(b, 3):
                rows.append(
                    e[:, a] * e[:, b] * e[:, c]
                    - sound * (e[:, a] * ident[b, c] + e[:, b] * ident[a, c] + e[:, c] * ident[a, b])
                )
    return np.stack([r / np.sqrt((r * r).sum()) for r in rows]).astype(np.float32)


def row_order(velocity):
    up = [(0, 0, 3), (0, 0, 2), (2, 0, 2), (-2, 0, 2), (0, 2, 2), (0, -2, 2), (0, 0, 1), (1, 1, 1)]
    mixed = [(1, -1, 1), (-1, 1, 1), (-1, -1, 1), (1, 0, 0)]
    level = [(0, 1, 0), (2, 0, 0), (0, 2, 0), (2, 2, 0), (2, -2, 0), (3, 0, 0), (0, 3, 0)]
    neg = lambda group: [tuple(-v for v in e) for e in group]
    order = up + mixed + neg(mixed) + neg(up) + level + [(0, 0, 0)] + neg(level)
    assert sorted(order) == sorted(velocity)
    return order


def tables():
    velocity = velocity_table()
    order = row_order(velocity)
    where = [velocity.index(e) for e in order]
    herm = hermite_table(velocity)[:, where]
    herm = np.concatenate([herm, np.zeros((MOM, 1), np.float32)], axis=1)
    bf = lambda a: np.asarray(jnp.asarray(a).astype(BF16).astype(F32))
    hi = bf(herm)
    mid = bf(herm - hi)
    low = bf(herm - hi - mid)
    thick = np.concatenate([hi, mid, low, np.zeros((4, ROWS), np.float32)])
    spread = np.zeros((64, 128), np.float32)
    for part in range(3):
        spread[:, part * ROWS : (part + 1) * ROWS] = thick
    for part in range(3):
        spread[60 + part, 120 + part] = 1.0
    final = np.zeros((24, 128), np.float32)
    final[:MOM, :ROWS] = herm
    final[:MOM, ROWS : 2 * ROWS] = herm
    final[MOM, 120] = 1.0
    pick = np.zeros((48, 128), np.float32)
    for row, q in enumerate(where):
        pick[row, q] = 1.0
    floats = np.zeros((320, 128), np.float32)
    floats[0:64] = spread
    floats[64:88] = final
    floats[88:136] = pick
    floats[136:184, :48] = pick.T[:48, :48]
    floats[184:224, :64] = thick.T
    ints = np.zeros((5, ROWS, 128), np.int32)
    for row, q in enumerate(where):
        ints[4, :, q] = row
    for row, e in enumerate(order):
        for back, sign in ((0, 1), (1, -1)):
            for lane in range(128):
                x, y = lane // 16, lane % 16
                source = ((x - sign * e[0]) % 16) * 16 + (y - sign * e[1]) % 16
                ints[2 * back, row, lane] = source % 128
                ints[2 * back + 1, row, lane] = source // 128
    ints[0, 39], ints[2, 39] = np.arange(128), np.arange(128)
    ints[4, :, Q:] = ROWS - 1
    return where, floats, ints


WHERE, FLOATS, INTS = tables()


def kernel(
    grid, scale, *refs
):
    (
    field_at, solid_at, cotangent_at, w_in_at, b_in_at, w_out_at, b_out_at, floats_at, ints_at, d_field, sums,
    field, solid, cotangent, w_in, b_in, w_out, b_out, floats, ints, by_q, in_sem, out_sem, pads, start, back_in, state, bounce, walls, xs, hid, dact, gbs, w_stack, w_trans, wo, wo_trans, bias, acc_in, acc_out,
    acc_b, parts, from_core, from_y, from_x, from_z, merged, final,
    halo_send, halo_recv, core_send, core_recv, y_send, y_recv, x_send, x_recv, z_send, z_recv, e_send, e_recv,
    ) = refs
    ny, nz, nx = grid
    me_s, me_x = lax.axis_index("space"), lax.axis_index("traj")
    core = lax.rem(me_s, 2)
    me_z = lax.rem(me_s // 2, nz)
    me_y = me_s // (2 * nz)
    n_space = ny * nz * 2
    up = (lax.rem(me_s + 1, n_space), me_x)
    down = (lax.rem(me_s + n_space - 1, n_space), me_x)
    place = lambda y, z, c: (y * nz + z) * 2 + c
    partner = (place(me_y, me_z, 1 - core), me_x)
    at_y = lambda k: (place(lax.rem(me_y + k, ny), me_z, core), me_x)
    at_z = lambda k: (place(me_y, lax.rem(me_z + k, nz), core), me_x)
    at_x = lambda k: (me_s, lax.rem(me_x + k, nx))
    peers = [up, down] + [at_y(k) for k in range(1, ny)] + [at_x(k) for k in range(1, nx)] + [at_z(k) for k in range(1, nz)]

    barrier = pltpu.get_barrier_semaphore()
    for peer in peers:
        pl.semaphore_signal(barrier, inc=1, device_id=peer, device_id_type=MESH)

    copies_in = [
        pltpu.make_async_copy(src, dst, in_sem.at[i])
        for i, (src, dst) in enumerate(
            [
                (floats_at, floats), (w_in_at, w_in), (b_in_at, b_in), (w_out_at, w_out), (b_out_at, b_out),
                (field_at, field), (solid_at, solid), (ints_at, ints), (cotangent_at, cotangent),
            ]
        )
    ]
    for copy in copies_in:
        copy.start()
    for copy in copies_in[:5]:
        copy.wait()

    w = w_in[...].astype(F32)
    b = b_in[...]
    b_hi = b.astype(BF16).astype(F32)
    b_mid = (b - b_hi).astype(BF16).astype(F32)
    b_low = b - b_hi - b_mid
    stack = jnp.concatenate([w, w, w, b_hi, b_mid, b_low, jnp.zeros((1, HID), F32)], axis=0)
    spread = floats[0:64, :].astype(BF16)
    full = jnp.dot(stack.T.astype(BF16), spread, preferred_element_type=F32)
    column = lax.broadcasted_iota(jnp.int32, (HID, 128), 1)
    low_part = full - full.astype(BF16).astype(F32)
    w_stack[...] = jnp.where((column >= 2 * ROWS) & (column < 3 * ROWS), low_part, full).astype(BF16)
    thick_t = floats[184:224, 0:64].astype(BF16)
    w_trans[...] = jnp.dot(thick_t, stack.astype(BF16), preferred_element_type=F32).astype(BF16)
    pick = floats[88:136, 0:Q].astype(BF16)
    by_row = jnp.dot(pick, w_out[...], preferred_element_type=F32)
    wo[...] = by_row.T.astype(BF16)
    wo_trans[...] = by_row[:ROWS].astype(BF16)
    bo = lax.dot_general(
        floats[88:136, 0:Q], jnp.broadcast_to(b_out[...], (8, Q)), NT, precision=lax.Precision.HIGHEST, preferred_element_type=F32
    )
    bias[...] = jnp.broadcast_to(bo[:ROWS, 0:1], (ROWS, PLANE))
    acc_b[...] = jnp.zeros((ROWS, PLANE), F32)

    zeros = jnp.zeros((CZ, 128), F32)

    def by_plane(source, rows):
        for half in range(2):
            lanes = slice(128 * half, 128 * half + 128)
            for row in range(ROWS):
                value = source[0, WHERE[row], :, lanes] if row < Q else zeros
                rows[half, pl.ds(row, CZ, stride=ROWS), :] = value

    copies_in[5].wait()
    by_plane(field, start)

    row8 = lax.broadcasted_iota(jnp.int32, (8, PLANE), 0)

    def wall_of(z):
        return walls[z] > 0

    def opposite(v):
        last = row8 == 7
        return jnp.concatenate(
            [
                v[16:24],
                jnp.concatenate([v[12:16], v[8:12]], axis=0),
                v[0:8],
                jnp.where(last, v[24:32], v[32:40]),
                jnp.where(last, v[32:40], v[24:32]),
            ],
            axis=0,
        )

    def select(wall, a, b):
        return jnp.concatenate([jnp.where(wall, a[8 * i : 8 * i + 8], b[8 * i : 8 * i + 8]) for i in range(5)], axis=0)

    def streamed(pad, z, sign):
        here = z + 3
        plane = lambda by, rows: pad[here - sign * by, rows, :]
        a, m, o, r = slice(0, 8), slice(8, 16), slice(16, 24), slice(24, 40)
        top = jnp.where(row8 == 0, plane(3, a), jnp.where(row8 < 6, plane(2, a), plane(1, a)))
        mix = jnp.where(row8 < 3, plane(1, m), jnp.where((row8 > 3) & (row8 < 7), plane(-1, m), plane(0, m)))
        low = jnp.where(row8 == 0, plane(-3, o), jnp.where(row8 < 6, plane(-2, o), plane(-1, o)))
        v = jnp.concatenate([top, mix, low, plane(0, r)], axis=0)
        which = 0 if sign == 1 else 2
        index, far = ints[which], ints[which + 1] > 0
        left = jnp.take_along_axis(v[:, 0:128], index, axis=1, mode="promise_in_bounds")
        right = jnp.take_along_axis(v[:, 128:256], index, axis=1, mode="promise_in_bounds")
        return jnp.concatenate([jnp.where(far, right, left), jnp.where(far, left, right)], axis=1)

    def cells_of(z):
        return slice(z * PLANE, z * PLANE + PLANE)

    def loaded(ref, z):
        rows = slice(z * ROWS, z * ROWS + ROWS)
        return jnp.concatenate([ref[0, rows, :], ref[1, rows, :]], axis=1)

    ones = jnp.ones((8, 2 * PLANE), F32)

    def side_by_side(parts):
        return jnp.concatenate(parts, axis=1)

    def forward_hidden(t, pair):
        values = []
        for z in pair:
            if t == 0:
                values.append(loaded(start, z))
            else:
                pad = pads.at[t]
                values.append(select(wall_of(z), opposite(pad[z + 3]), streamed(pad, z, 1)))
        v = side_by_side(values)
        v_hi = v.astype(BF16).astype(F32)
        x = jnp.concatenate([v_hi, v - v_hi, v_hi, ones], axis=0).astype(BF16)
        for i, z in enumerate(pair):
            xs[t, :, cells_of(z)] = x[:, PLANE * i : PLANE * i + PLANE]
        halves = []
        for c in range(2):
            rows = slice(256 * c, 256 * c + 256)
            act = jnp.dot(w_stack[rows, :], x, preferred_element_type=F32)
            h = jnp.tanh(act).astype(BF16)
            for i, z in enumerate(pair):
                hid[t, rows, cells_of(z)] = h[:, PLANE * i : PLANE * i + PLANE]
            halves.append(h)
        return v, jnp.concatenate(halves, axis=0)

    def forward_change(t, pair, done):
        if t < 2:
            v, h = done
            change = jnp.dot(wo_trans[...], h, preferred_element_type=F32)
            for i, z in enumerate(pair):
                cut = slice(PLANE * i, PLANE * i + PLANE)
                pads[t + 1, z + 3] = v[:, cut] + change[:, cut] + bias[...]

    def outgoing(z, g, slot):
        wall = wall_of(z)
        nothing = jnp.zeros((ROWS, PLANE), F32)
        bounce[z] = select(wall, opposite(g), nothing)
        pads[slot, z + 3] = select(wall, nothing, g)

    def backward_hidden(t, pair):
        slot = (4, 3, 0)[t]
        posts = [streamed(pads.at[slot], z, -1) + bounce[z] for z in pair]
        acc_b[...] += posts[0] + posts[1]
        g_post = side_by_side(posts)
        gb = jnp.concatenate([g_post, jnp.zeros((8, 2 * PLANE), F32)], axis=0).astype(BF16)
        for i, z in enumerate(pair):
            gbs[:, cells_of(z)] = gb[:, PLANE * i : PLANE * i + PLANE]
        halves = []
        for c in range(2):
            rows = slice(256 * c, 256 * c + 256)
            dh = jnp.dot(wo[rows, :], gb, preferred_element_type=F32)
            h = side_by_side([hid[t, rows, cells_of(z)] for z in pair]).astype(F32)
            da = (dh * (1.0 - h * h)).astype(BF16)
            for i, z in enumerate(pair):
                dact[rows, cells_of(z)] = da[:, PLANE * i : PLANE * i + PLANE]
            halves.append(da)
        return g_post, jnp.concatenate(halves, axis=0)

    def backward_change(t, pair, done):
        g_post, da = done
        g = g_post + jnp.dot(w_trans[...], da, preferred_element_type=F32)
        for i, z in enumerate(pair):
            cut = slice(PLANE * i, PLANE * i + PLANE)
            if t > 0:
                outgoing(z, g[:, cut], 5 - t)
            else:
                state[z] = g[:, cut]

    def grads(t):
        g_in = lax.dot_general(xs[t], dact[...], NT, preferred_element_type=F32)
        g_out = lax.dot_general(gbs[...], hid[t], NT, preferred_element_type=F32)
        if t == 2:
            acc_in[...] = g_in
            acc_out[...] = g_out
        else:
            acc_in[...] += g_in
            acc_out[...] += g_out

    def halo(slot, sign):
        first, second = (up, down) if sign == 1 else (down, up)
        pad = pads.at[slot]
        if sign == 1:
            moves = [
                (pad.at[10, 0:16], pad.at[2, 0:16], up),
                (pad.at[8:10, 0:8], pad.at[0:2, 0:8], up),
                (pad.at[3, 8:24], pad.at[11, 8:24], down),
                (pad.at[4:6, 16:24], pad.at[12:14, 16:24], down),
            ]
        else:
            moves = [
                (pad.at[3, 0:16], pad.at[11, 0:16], down),
                (pad.at[4:6, 0:8], pad.at[12:14, 0:8], down),
                (pad.at[10, 8:24], pad.at[2, 8:24], up),
                (pad.at[8:10, 16:24], pad.at[0:2, 16:24], up),
            ]
        return [
            pltpu.make_async_remote_copy(
                src_ref=src, dst_ref=dst, send_sem=halo_send.at[slot, i], recv_sem=halo_recv.at[slot, i],
                device_id=to, device_id_type=MESH,
            )
            for i, (src, dst, to) in enumerate(moves)
        ]

    def begin(copies):
        for copy in copies:
            copy.start()

    def end(copies):
        for copy in copies:
            copy.wait_recv()

    MIDDLE, OUTER = [(3, 4)], [(0, 1), (2, 5), (6, 7)]

    def in_turn(first, second, t, pairs, before=None):
        done = None
        for pair in pairs:
            if before is not None and pair in OUTER:
                end(before)
                before = None
            now = first(t, pair)
            if done is not None:
                second(t, *done)
            done = (pair, now)
        second(t, *done)

    def forwards(t, before=None):
        in_turn(forward_hidden, forward_change, t, MIDDLE + OUTER, before)

    def backwards(t, before=None):
        in_turn(backward_hidden, backward_change, t, MIDDLE + OUTER, before)

    forwards(0)
    for copy in copies_in[6:8]:
        copy.wait()
    pl.semaphore_wait(barrier, len(peers))
    copy_1 = halo(1, 1)
    begin(copy_1)
    for z in range(CZ):
        walls[z] = jnp.broadcast_to(solid[0, z : z + 1, :], (8, PLANE))
    copies_in[8].wait()
    by_plane(cotangent, back_in)
    for z in range(CZ):
        outgoing(z, loaded(back_in, z), 0)
    copy_0 = halo(0, -1)
    begin(copy_0)
    forwards(1, copy_1)
    copy_2 = halo(2, 1)
    begin(copy_2)
    forwards(2, copy_2)
    backwards(2, copy_0)
    copy_3 = halo(3, -1)
    begin(copy_3)
    grads(2)
    backwards(1, copy_3)
    copy_4 = halo(4, -1)
    begin(copy_4)
    grads(1)
    backwards(0, copy_4)
    grads(0)

    def two(v):
        v_hi = v.astype(BF16).astype(F32)
        return v_hi, v - v_hi

    a_hi, a_low = two(acc_in[...])
    f_hi, f_low = two(floats[64:88, :])
    left = jnp.concatenate([f_hi, f_hi], axis=1).astype(BF16)
    right = jnp.concatenate([a_hi, a_low], axis=0).astype(BF16)
    upper = jnp.dot(left, right, preferred_element_type=F32)
    upper = upper + jnp.dot(f_low.astype(BF16), a_hi.astype(BF16), preferred_element_type=F32)
    b_hi, b_low = two(acc_b[...])
    pair = jnp.concatenate([b_hi, jnp.zeros((24, PLANE), F32), b_low, jnp.zeros((24, PLANE), F32)], axis=0).astype(BF16)
    line = lax.dot_general(jnp.ones((8, PLANE), BF16), pair, NT, preferred_element_type=F32)
    line = line + jnp.concatenate([line[:, 64:], line[:, :64]], axis=1)
    line = jnp.take_along_axis(line, ints[4, 0:8], axis=1, mode="promise_in_bounds")
    for i in range(3):
        for j in range(4):
            parts[4 * i + j] = upper[8 * i : 8 * i + 8, 128 * j : 128 * j + 128]
    for row in range(Q):
        i, k = divmod(WHERE[row] + 24, 8)
        for j in range(4):
            parts[4 * i + j, k : k + 1, :] = acc_out[row : row + 1, 128 * j : 128 * j + 128]
    for j in range(4):
        parts[28 + j, 7:8, :] = line[0:1] if j == 0 else jnp.zeros((1, 128), F32)

    def remote(src, dst, send, recv, to):
        return pltpu.make_async_remote_copy(
            src_ref=src, dst_ref=dst, send_sem=send, recv_sem=recv, device_id=to, device_id_type=MESH
        )

    mine = pl.multiple_of(core * 16, 16)
    other = pl.multiple_of((1 - core) * 16, 16)
    swap = remote(parts.at[pl.ds(other, 16)], from_core, core_send.at[0], core_recv.at[0], partner)
    swap.start()

    for half in range(2):
        for z in range(CZ):
            start[half, ROWS * z : ROWS * z + ROWS, :] = state[z, :, 128 * half : 128 * half + 128]
    for half in range(2):
        for row in range(Q):
            by_q[0, WHERE[row], :, 128 * half : 128 * half + 128] = start[half, pl.ds(row, CZ, stride=ROWS), :]

    field_out = pltpu.make_async_copy(by_q, d_field, out_sem.at[0])
    field_out.start()
    swap.wait_recv()
    merged[...] = parts[pl.ds(mine, 16)] + from_core[...]
    per = 16 // ny
    scatter = []
    for k in range(ny - 1, 0, -1):
        piece = lax.rem(me_y + k, ny) * per
        scatter.append(remote(merged.at[pl.ds(piece, per)], from_y.at[k - 1], y_send.at[k - 1], y_recv.at[k - 1], at_y(k)))
    begin(scatter)
    end(scatter)
    total = merged[pl.ds(me_y * per, per)]
    for k in range(ny - 1):
        total = total + from_y[k]

    from_x[me_x] = total
    across = [
        remote(from_x.at[me_x], from_x.at[me_x], x_send.at[k - 1], x_recv.at[k - 1], at_x(k)) for k in range(1, nx)
    ]
    begin(across)
    end(across)
    total = from_x[0]
    for k in range(1, nx):
        total = total + from_x[k]

    from_z[me_z] = total
    far_first = sorted(range(1, nz), key=lambda k: -min(k, nz - k))
    along = [
        remote(from_z.at[me_z], from_z.at[me_z], z_send.at[k - 1], z_recv.at[k - 1], at_z(k)) for k in far_first
    ]
    begin(along)
    end(along)
    total = from_z[0]
    for k in range(1, nz):
        total = total + from_z[k]

    own = pl.ds(core * 16 + me_y * per, per)
    final[own] = total * scale
    spread_out = [
        remote(final.at[own], final.at[own], e_send.at[k - 1], e_recv.at[k - 1], at_y(k)) for k in range(ny - 1, 0, -1)
    ]
    begin(spread_out)
    end(spread_out)
    give = remote(final.at[pl.ds(mine, 16)], final.at[pl.ds(mine, 16)], core_send.at[1], core_recv.at[1], partner)
    give.start()
    give.wait_recv()
    sums_out = pltpu.make_async_copy(final, sums, out_sem.at[1])
    sums_out.start()
    for copies in (copy_0, copy_1, copy_2, copy_3, copy_4, [swap], scatter, across, along, spread_out, [give]):
        for copy in copies:
            copy.wait_send()
    field_out.wait()
    sums_out.wait()


def write_out(field_at, sums_at, d_field, g_w_in, g_b_in, g_w_out, g_b_out, field, sums, a, b, c, d, sem):
    field_in = pltpu.make_async_copy(field_at, field, sem.at[0])
    sums_in = pltpu.make_async_copy(sums_at, sums, sem.at[1])
    sums_in.start()
    field_in.start()
    sums_in.wait()
    for j in range(4):
        cut = slice(128 * j, 128 * j + 128)
        a[0:8, cut] = sums[j]
        a[8:16, cut] = sums[4 + j]
        a[16:20, cut] = sums[8 + j, 0:4]
        b[:, cut] = sums[8 + j, 4:5]
        for i in range(3, 7):
            c[8 * i - 24 : 8 * i - 16, cut] = sums[4 * i + j]
        c[32:39, cut] = sums[28 + j, 0:7]
    d[...] = sums[28, 7:8, 0:Q]
    small = [
        pltpu.make_async_copy(src, dst, sem.at[i])
        for i, (src, dst) in enumerate([(a, g_w_in), (b, g_b_in), (c, g_w_out), (d, g_b_out)], 2)
    ]
    for copy in small:
        copy.start()
    field_in.wait()
    big = pltpu.make_async_copy(field, d_field, sem.at[6])
    big.start()
    for copy in small + [big]:
        copy.wait()


def solution(mesh):
    n_space, nx = mesh.shape["space"], mesh.shape["traj"]
    ny = 8 if n_space % 16 == 0 else 2
    nz = n_space // (2 * ny)
    scale = 1.0 / math.sqrt(float(n_space * nx * CELLS * STEPS))
    per = 16 // ny
    hbm = pl.BlockSpec(memory_space=pltpu.HBM)
    dma = pltpu.SemaphoreType.DMA

    def per_device(field, solid, cotangent, w_in, b_in, w_out, b_out):
        def body(*refs):
            kernel((ny, nz, nx), scale, *refs)

        d_field, sums = pl.pallas_call(
            body,
            out_shape=(jax.ShapeDtypeStruct(field.shape, F32), jax.ShapeDtypeStruct((32, 8, 128), F32)),
            in_specs=[hbm] * 9,
            out_specs=(hbm, hbm),
            scratch_shapes=[
                pltpu.VMEM(field.shape, F32),
                pltpu.VMEM(solid.shape, jnp.int32),
                pltpu.VMEM(field.shape, F32),
                pltpu.VMEM(w_in.shape, BF16),
                pltpu.VMEM((1, HID), F32),
                pltpu.VMEM((Q, HID), BF16),
                pltpu.VMEM((1, Q), F32),
                pltpu.VMEM(FLOATS.shape, F32),
                pltpu.VMEM(INTS.shape, jnp.int32),
                pltpu.VMEM(field.shape, F32),
                dma((9,)),
                dma((2,)),
                pltpu.VMEM((5, CZ + 6, ROWS, PLANE), F32),
                pltpu.VMEM((2, CZ * ROWS, 128), F32),
                pltpu.VMEM((2, CZ * ROWS, 128), F32),
                pltpu.VMEM((CZ, ROWS, PLANE), F32),
                pltpu.VMEM((CZ, ROWS, PLANE), F32),
                pltpu.VMEM((CZ, 8, PLANE), jnp.int32),
                pltpu.VMEM((STEPS, 128, CELLS), BF16),
                pltpu.VMEM((STEPS, HID, CELLS), BF16),
                pltpu.VMEM((HID, CELLS), BF16),
                pltpu.VMEM((48, CELLS), BF16),
                pltpu.VMEM((HID, 128), BF16),
                pltpu.VMEM((ROWS, HID), BF16),
                pltpu.VMEM((HID, 48), BF16),
                pltpu.VMEM((ROWS, HID), BF16),
                pltpu.VMEM((ROWS, PLANE), F32),
                pltpu.VMEM((128, HID), F32),
                pltpu.VMEM((48, HID), F32),
                pltpu.VMEM((ROWS, PLANE), F32),
                pltpu.VMEM((32, 8, 128), F32),
                pltpu.VMEM((16, 8, 128), F32),
                pltpu.VMEM((ny - 1, per, 8, 128), F32),
                pltpu.VMEM((nx, per, 8, 128), F32),
                pltpu.VMEM((nz, per, 8, 128), F32),
                pltpu.VMEM((16, 8, 128), F32),
                pltpu.VMEM((32, 8, 128), F32),
                dma((5, 4)), dma((5, 4)), dma((2,)), dma((2,)), dma((ny - 1,)), dma((ny - 1,)),
                dma((max(nx - 1, 1),)), dma((max(nx - 1, 1),)), dma((nz - 1,)), dma((nz - 1,)), dma((ny - 1,)), dma((ny - 1,)),
            ],
            compiler_params=pltpu.CompilerParams(collective_id=0, has_side_effects=True, vmem_limit_bytes=62 << 20),
            name="adjoint",
        )(field, solid, cotangent, w_in, b_in.reshape(1, HID), w_out.T, b_out.reshape(1, Q), jnp.asarray(FLOATS), jnp.asarray(INTS))
        d_field, g_w_in, g_b_in, g_w_out, g_b_out = pl.pallas_call(
            write_out,
            out_shape=(
                jax.ShapeDtypeStruct(field.shape, F32),
                jax.ShapeDtypeStruct((MOM, HID), F32),
                jax.ShapeDtypeStruct((1, HID), F32),
                jax.ShapeDtypeStruct((Q, HID), F32),
                jax.ShapeDtypeStruct((1, Q), F32),
            ),
            in_specs=[hbm, hbm],
            out_specs=(hbm,) * 5,
            scratch_shapes=[
                pltpu.VMEM(field.shape, F32), pltpu.VMEM((32, 8, 128), F32),
                pltpu.VMEM((MOM, HID), F32), pltpu.VMEM((1, HID), F32), pltpu.VMEM((Q, HID), F32), pltpu.VMEM((1, Q), F32),
                dma((7,)),
            ],
            compiler_params=pltpu.CompilerParams(vmem_limit_bytes=62 << 20),
            name="write_out",
        )(d_field, sums)
        return d_field, g_w_in, g_b_in.reshape(HID), g_w_out.T, g_b_out.reshape(Q)

    return jax.shard_map(
        per_device,
        mesh=mesh,
        in_specs=(P("traj", None, "space", None), P("traj", "space", None), P("traj", None, "space", None), P(), P(), P(), P()),
        out_specs=(P("traj", None, "space", None), P(), P(), P(), P()),
        check_vma=False,
    )
```

```python
import math

import jax
import jax.numpy as jnp
import numpy as np
from jax import lax
from jax.experimental import pallas as pl
from jax.experimental.pallas import tpu as pltpu
from jax.sharding import PartitionSpec as P

STEPS = 3
Q = 39
MOM = 20
HID = 512
CZ = 8
PLANE = 256
ROWS = 40
CELLS = CZ * PLANE
MESH = pl.DeviceIdType.MESH
F32 = jnp.float32
BF16 = jnp.bfloat16
NT = (((1,), (1,)), ((), ()))


def velocity_table():
    rows = [(0, 0, 0)]
    for axis_one in range(3):
        for sign in (1, -1):
            entry = [0, 0, 0]
            entry[axis_one] = sign
            rows.append(tuple(entry))
    for along_x in (1, -1):
        for along_y in (1, -1):
            for along_z in (1, -1):
                rows.append((along_x, along_y, along_z))
    for axis_one in range(3):
        for sign in (1, -1):
            entry = [0, 0, 0]
            entry[axis_one] = 2 * sign
            rows.append(tuple(entry))
    for first, second in ((0, 1), (0, 2), (1, 2)):
        for sign_one in (2, -2):
            for sign_two in (2, -2):
                entry = [0, 0, 0]
                entry[first] = sign_one
                entry[second] = sign_two
                rows.append(tuple(entry))
    for axis_one in range(3):
        for sign in (1, -1):
            entry = [0, 0, 0]
            entry[axis_one] = 3 * sign
            rows.append(tuple(entry))
    return rows


def hermite_table(velocity):
    sound = 2.0 / 3.0
    e = np.asarray(velocity, np.float64)
    ident = np.eye(3)
    rows = [np.ones(len(velocity))]
    for a in range(3):
        rows.append(e[:, a])
    for a in range(3):
        for b in range(a, 3):
            rows.append(e[:, a] * e[:, b] - sound * ident[a, b])
    for a in range(3):
        for b in range(a, 3):
            for c in range(b, 3):
                rows.append(
                    e[:, a] * e[:, b] * e[:, c]
                    - sound * (e[:, a] * ident[b, c] + e[:, b] * ident[a, c] + e[:, c] * ident[a, b])
                )
    return np.stack([r / np.sqrt((r * r).sum()) for r in rows]).astype(np.float32)


def row_order(velocity):
    up = [(0, 0, 3), (0, 0, 2), (2, 0, 2), (-2, 0, 2), (0, 2, 2), (0, -2, 2), (0, 0, 1), (1, 1, 1)]
    mixed = [(1, -1, 1), (-1, 1, 1), (-1, -1, 1), (1, 0, 0)]
    level = [(0, 1, 0), (2, 0, 0), (0, 2, 0), (2, 2, 0), (2, -2, 0), (3, 0, 0), (0, 3, 0)]
    neg = lambda group: [tuple(-v for v in e) for e in group]
    order = up + mixed + neg(mixed) + neg(up) + level + [(0, 0, 0)] + neg(level)
    assert sorted(order) == sorted(velocity)
    return order


def tables():
    velocity = velocity_table()
    order = row_order(velocity)
    where = [velocity.index(e) for e in order]
    herm = hermite_table(velocity)[:, where]
    herm = np.concatenate([herm, np.zeros((MOM, 1), np.float32)], axis=1)
    bf = lambda a: np.asarray(jnp.asarray(a).astype(BF16).astype(F32))
    hi = bf(herm)
    mid = bf(herm - hi)
    low = bf(herm - hi - mid)
    thick = np.concatenate([hi, mid, low, np.zeros((4, ROWS), np.float32)])
    spread = np.zeros((64, 128), np.float32)
    for part in range(3):
        spread[:, part * ROWS : (part + 1) * ROWS] = thick
    for part in range(3):
        spread[60 + part, 120 + part] = 1.0
    final = np.zeros((24, 128), np.float32)
    final[:MOM, :ROWS] = herm
    final[:MOM, ROWS : 2 * ROWS] = herm
    final[MOM, 120] = 1.0
    pick = np.zeros((48, 128), np.float32)
    for row, q in enumerate(where):
        pick[row, q] = 1.0
    floats = np.zeros((320, 128), np.float32)
    floats[0:64] = spread
    floats[64:88] = final
    floats[88:136] = pick
    floats[136:184, :48] = pick.T[:48, :48]
    floats[184:224, :64] = thick.T
    ints = np.zeros((5, ROWS, 128), np.int32)
    for row, q in enumerate(where):
        ints[4, :, q] = row
    for row, e in enumerate(order):
        for back, sign in ((0, 1), (1, -1)):
            for lane in range(128):
                x, y = lane // 16, lane % 16
                source = ((x - sign * e[0]) % 16) * 16 + (y - sign * e[1]) % 16
                ints[2 * back, row, lane] = source % 128
                ints[2 * back + 1, row, lane] = source // 128
    ints[0, 39], ints[2, 39] = np.arange(128), np.arange(128)
    ints[4, :, Q:] = ROWS - 1
    return where, floats, ints


WHERE, FLOATS, INTS = tables()


def kernel(
    grid, scale, *refs
):
    (
    field_at, solid_at, cotangent_at, w_in_at, b_in_at, w_out_at, b_out_at, floats_at, ints_at, d_field, sums,
    field, solid, cotangent, w_in, b_in, w_out, b_out, floats, ints, by_q, in_sem, out_sem, pads, start, back_in, state, bounce, walls, xs, hid, dact, dhs, gbs, w_stack, w_trans, wo, wo_trans, bias, acc_in, acc_out,
    acc_b, parts, from_core, from_y, from_x, from_z, merged, final,
    halo_send, halo_recv, core_send, core_recv, y_send, y_recv, x_send, x_recv, z_send, z_recv, e_send, e_recv, g_send, g_recv,
    ) = refs
    ny, nz, nx = grid
    me_s, me_x = lax.axis_index("space"), lax.axis_index("traj")
    core = lax.rem(me_s, 2)
    me_z = lax.rem(me_s // 2, nz)
    me_y = me_s // (2 * nz)
    n_space = ny * nz * 2
    up = (lax.rem(me_s + 1, n_space), me_x)
    down = (lax.rem(me_s + n_space - 1, n_space), me_x)
    place = lambda y, z, c: (y * nz + z) * 2 + c
    partner = (place(me_y, me_z, 1 - core), me_x)
    at_y = lambda k: (place(lax.rem(me_y + k, ny), me_z, core), me_x)
    at_z = lambda k: (place(me_y, lax.rem(me_z + k, nz), core), me_x)
    at_x = lambda k: (me_s, lax.rem(me_x + k, nx))
    peers = [up, down] + [at_y(k) for k in range(1, ny)] + [at_x(k) for k in range(1, nx)] + [at_z(k) for k in range(1, nz)]

    barrier = pltpu.get_barrier_semaphore()
    for peer in peers:
        pl.semaphore_signal(barrier, inc=1, device_id=peer, device_id_type=MESH)

    copies_in = [
        pltpu.make_async_copy(src, dst, in_sem.at[i])
        for i, (src, dst) in enumerate(
            [
                (floats_at, floats), (w_in_at, w_in), (b_in_at, b_in), (w_out_at, w_out), (b_out_at, b_out),
                (field_at, field), (solid_at, solid), (ints_at, ints), (cotangent_at, cotangent),
            ]
        )
    ]
    for copy in copies_in:
        copy.start()
    for copy in copies_in[:5]:
        copy.wait()

    w = w_in[...].astype(F32)
    b = b_in[...]
    b_hi = b.astype(BF16).astype(F32)
    b_mid = (b - b_hi).astype(BF16).astype(F32)
    b_low = b - b_hi - b_mid
    stack = jnp.concatenate([w, w, w, b_hi, b_mid, b_low, jnp.zeros((1, HID), F32)], axis=0)
    spread = floats[0:64, :].astype(BF16)
    full = jnp.dot(stack.T.astype(BF16), spread, preferred_element_type=F32)
    column = lax.broadcasted_iota(jnp.int32, (HID, 128), 1)
    low_part = full - full.astype(BF16).astype(F32)
    w_stack[...] = jnp.where((column >= 2 * ROWS) & (column < 3 * ROWS), low_part, full).astype(BF16)
    thick_t = floats[184:224, 0:64].astype(BF16)
    w_trans[...] = jnp.dot(thick_t, stack.astype(BF16), preferred_element_type=F32).astype(BF16)
    pick = floats[88:136, 0:Q].astype(BF16)
    by_row = jnp.dot(pick, w_out[...], preferred_element_type=F32)
    wo[...] = by_row.T.astype(BF16)
    wo_trans[...] = by_row[:ROWS].astype(BF16)
    bo = lax.dot_general(
        floats[88:136, 0:Q], jnp.broadcast_to(b_out[...], (8, Q)), NT, precision=lax.Precision.HIGHEST, preferred_element_type=F32
    )
    bias[...] = jnp.broadcast_to(bo[:ROWS, 0:1], (ROWS, PLANE))
    acc_b[...] = jnp.zeros((ROWS, PLANE), F32)

    zeros = jnp.zeros((CZ, 128), F32)

    def by_plane(source, rows):
        for half in range(2):
            lanes = slice(128 * half, 128 * half + 128)
            for row in range(ROWS):
                value = source[0, WHERE[row], :, lanes] if row < Q else zeros
                rows[half, pl.ds(row, CZ, stride=ROWS), :] = value

    copies_in[5].wait()
    by_plane(field, start)

    row8 = lax.broadcasted_iota(jnp.int32, (8, PLANE), 0)

    def wall_of(z):
        return walls[z] > 0

    def opposite(v):
        last = row8 == 7
        return jnp.concatenate(
            [
                v[16:24],
                jnp.concatenate([v[12:16], v[8:12]], axis=0),
                v[0:8],
                jnp.where(last, v[24:32], v[32:40]),
                jnp.where(last, v[32:40], v[24:32]),
            ],
            axis=0,
        )

    def select(wall, a, b):
        return jnp.concatenate([jnp.where(wall, a[8 * i : 8 * i + 8], b[8 * i : 8 * i + 8]) for i in range(5)], axis=0)

    def streamed(pad, z, sign):
        here = z + 3
        plane = lambda by, rows: pad[here - sign * by, rows, :]
        a, m, o, r = slice(0, 8), slice(8, 16), slice(16, 24), slice(24, 40)
        top = jnp.where(row8 == 0, plane(3, a), jnp.where(row8 < 6, plane(2, a), plane(1, a)))
        mix = jnp.where(row8 < 3, plane(1, m), jnp.where((row8 > 3) & (row8 < 7), plane(-1, m), plane(0, m)))
        low = jnp.where(row8 == 0, plane(-3, o), jnp.where(row8 < 6, plane(-2, o), plane(-1, o)))
        v = jnp.concatenate([top, mix, low, plane(0, r)], axis=0)
        which = 0 if sign == 1 else 2
        index, far = ints[which], ints[which + 1] > 0
        left = jnp.take_along_axis(v[:, 0:128], index, axis=1, mode="promise_in_bounds")
        right = jnp.take_along_axis(v[:, 128:256], index, axis=1, mode="promise_in_bounds")
        return jnp.concatenate([jnp.where(far, right, left), jnp.where(far, left, right)], axis=1)

    def cells_of(z):
        return slice(z * PLANE, z * PLANE + PLANE)

    def loaded(ref, z):
        rows = slice(z * ROWS, z * ROWS + ROWS)
        return jnp.concatenate([ref[0, rows, :], ref[1, rows, :]], axis=1)

    ones = jnp.ones((8, 2 * PLANE), F32)

    def side_by_side(parts):
        return jnp.concatenate(parts, axis=1)

    def forward_hidden(t, pair):
        values = []
        for z in pair:
            if t == 0:
                values.append(loaded(start, z))
            else:
                pad = pads.at[t]
                values.append(select(wall_of(z), opposite(pad[z + 3]), streamed(pad, z, 1)))
        v = side_by_side(values)
        v_hi = v.astype(BF16).astype(F32)
        x = jnp.concatenate([v_hi, v - v_hi, v_hi, ones], axis=0).astype(BF16)
        for i, z in enumerate(pair):
            xs[t, :, cells_of(z)] = x[:, PLANE * i : PLANE * i + PLANE]
        halves = []
        for c in range(2):
            rows = slice(256 * c, 256 * c + 256)
            act = jnp.dot(w_stack[rows, :], x, preferred_element_type=F32)
            wide = jnp.tanh(act)
            h = wide.astype(BF16)
            for i, z in enumerate(pair):
                hid[t, rows, cells_of(z)] = h[:, PLANE * i : PLANE * i + PLANE]
            if t == 2:
                wide = h.astype(F32)
                dh = side_by_side([dhs[rows, cells_of(z)] for z in pair]).astype(F32)
                h = (dh * (1.0 - wide * wide)).astype(BF16)
                for i, z in enumerate(pair):
                    dact[rows, cells_of(z)] = h[:, PLANE * i : PLANE * i + PLANE]
            halves.append(h)
        return v, jnp.concatenate(halves, axis=0)

    def forward_change(t, pair, done):
        if t == 2:
            g = side_by_side([state[z] for z in pair])
            backward_change(2, pair, (g, done[1]))
        else:
            v, h = done
            change = jnp.dot(wo_trans[...], h, preferred_element_type=F32)
            for i, z in enumerate(pair):
                cut = slice(PLANE * i, PLANE * i + PLANE)
                pads[t + 1, z + 3] = v[:, cut] + change[:, cut] + bias[...]

    def outgoing(z, g, slot):
        wall = wall_of(z)
        nothing = jnp.zeros((ROWS, PLANE), F32)
        bounce[z] = select(wall, opposite(g), nothing)
        pads[slot, z + 3] = select(wall, nothing, g)

    def backward_post(t, pair):
        slot = (4, 3, 0)[t]
        posts = [streamed(pads.at[slot], z, -1) + bounce[z] for z in pair]
        acc_b[...] += posts[0] + posts[1]
        g_post = side_by_side(posts)
        gb = jnp.concatenate([g_post, jnp.zeros((8, 2 * PLANE), F32)], axis=0).astype(BF16)
        for i, z in enumerate(pair):
            gbs[:, cells_of(z)] = gb[:, PLANE * i : PLANE * i + PLANE]
            if t != 1:
                state[z] = posts[i]
        return g_post, gb

    def backward_ahead(pair):
        g_post, gb = backward_post(2, pair)
        for c in range(2):
            rows = slice(256 * c, 256 * c + 256)
            dh = jnp.dot(wo[rows, :], gb, preferred_element_type=F32).astype(BF16)
            for i, z in enumerate(pair):
                dhs[rows, cells_of(z)] = dh[:, PLANE * i : PLANE * i + PLANE]

    def backward_hidden(t, pair):
        g_post, gb = backward_post(t, pair)
        halves = []
        for c in range(2):
            rows = slice(256 * c, 256 * c + 256)
            dh = jnp.dot(wo[rows, :], gb, preferred_element_type=F32)
            h = side_by_side([hid[t, rows, cells_of(z)] for z in pair]).astype(F32)
            da = (dh * (1.0 - h * h)).astype(BF16)
            for i, z in enumerate(pair):
                dact[rows, cells_of(z)] = da[:, PLANE * i : PLANE * i + PLANE]
            halves.append(da)
        return g_post, jnp.concatenate(halves, axis=0)

    def backward_field(pair):
        da = side_by_side([dact[:, cells_of(z)] for z in pair])
        change = jnp.dot(w_trans[...], da, preferred_element_type=F32)
        for i, z in enumerate(pair):
            g = state[z] + change[:, PLANE * i : PLANE * i + PLANE]
            for half in range(2):
                start[half, ROWS * z : ROWS * z + ROWS, :] = g[:, 128 * half : 128 * half + 128]

    def backward_change(t, pair, done):
        g_post, da = done
        g = g_post + jnp.dot(w_trans[...], da, preferred_element_type=F32)
        for i, z in enumerate(pair):
            cut = slice(PLANE * i, PLANE * i + PLANE)
            outgoing(z, g[:, cut], 5 - t)

    def grads(t):
        g_in = lax.dot_general(xs[t], dact[...], NT, preferred_element_type=F32)
        g_out = lax.dot_general(gbs[...], hid[t], NT, preferred_element_type=F32)
        if t == 2:
            acc_in[...] = g_in
            acc_out[...] = g_out
        else:
            acc_in[...] += g_in
            acc_out[...] += g_out

    def halo(slot, sign):
        first, second = (up, down) if sign == 1 else (down, up)
        pad = pads.at[slot]
        if sign == 1:
            moves = [
                (pad.at[10, 0:16], pad.at[2, 0:16], up),
                (pad.at[8:10, 0:8], pad.at[0:2, 0:8], up),
                (pad.at[3, 8:24], pad.at[11, 8:24], down),
                (pad.at[4:6, 16:24], pad.at[12:14, 16:24], down),
            ]
        else:
            moves = [
                (pad.at[3, 0:16], pad.at[11, 0:16], down),
                (pad.at[4:6, 0:8], pad.at[12:14, 0:8], down),
                (pad.at[10, 8:24], pad.at[2, 8:24], up),
                (pad.at[8:10, 16:24], pad.at[0:2, 16:24], up),
            ]
        return [
            pltpu.make_async_remote_copy(
                src_ref=src, dst_ref=dst, send_sem=halo_send.at[slot, i], recv_sem=halo_recv.at[slot, i],
                device_id=to, device_id_type=MESH,
            )
            for i, (src, dst, to) in enumerate(moves)
        ]

    def begin(copies):
        for copy in copies:
            copy.start()

    def end(copies):
        for copy in copies:
            copy.wait_recv()

    MIDDLE, OUTER = [(3, 4)], [(0, 1), (2, 5), (6, 7)]

    def in_turn(first, second, t, pairs, before=None):
        done = None
        for pair in pairs:
            if before is not None and pair in OUTER:
                end(before)
                before = None
            now = first(t, pair)
            if done is not None:
                second(t, *done)
            done = (pair, now)
        second(t, *done)

    def forwards(t, pairs, before=None):
        in_turn(forward_hidden, forward_change, t, pairs, before)

    def nothing(t, pair, done):
        pass

    forwards(0, OUTER)
    for copy in copies_in[6:8]:
        copy.wait()
    pl.semaphore_wait(barrier, len(peers))
    copy_1 = halo(1, 1)
    begin(copy_1)
    for z in range(CZ):
        walls[z] = jnp.broadcast_to(solid[0, z : z + 1, :], (8, PLANE))
    copies_in[8].wait()
    by_plane(cotangent, back_in)
    for z in range(CZ):
        outgoing(z, loaded(back_in, z), 0)
    copy_0 = halo(0, -1)
    begin(copy_0)
    forwards(0, MIDDLE)
    forwards(1, MIDDLE + OUTER, copy_1)
    copy_2 = halo(2, 1)
    begin(copy_2)
    end(copy_0)
    for pair in MIDDLE + OUTER:
        backward_ahead(pair)
    end(copy_2)
    forwards(2, OUTER)
    copy_3 = halo(3, -1)
    begin(copy_3)
    forwards(2, MIDDLE)
    grads(2)
    in_turn(backward_hidden, backward_change, 1, MIDDLE + OUTER, copy_3)
    copy_4 = halo(4, -1)
    begin(copy_4)
    grads(1)
    in_turn(backward_hidden, nothing, 0, MIDDLE + OUTER, copy_4)
    grads(0)

    def two(v):
        v_hi = v.astype(BF16).astype(F32)
        return v_hi, v - v_hi

    a_hi, a_low = two(acc_in[...])
    f_hi, f_low = two(floats[64:88, :])
    left = jnp.concatenate([f_hi, f_hi], axis=1).astype(BF16)
    right = jnp.concatenate([a_hi, a_low], axis=0).astype(BF16)
    upper = jnp.dot(left, right, preferred_element_type=F32)
    upper = upper + jnp.dot(f_low.astype(BF16), a_hi.astype(BF16), preferred_element_type=F32)
    b_hi, b_low = two(acc_b[...])
    pair = jnp.concatenate([b_hi, jnp.zeros((24, PLANE), F32), b_low, jnp.zeros((24, PLANE), F32)], axis=0).astype(BF16)
    line = lax.dot_general(jnp.ones((8, PLANE), BF16), pair, NT, preferred_element_type=F32)
    line = line + jnp.concatenate([line[:, 64:], line[:, :64]], axis=1)
    line = jnp.take_along_axis(line, ints[4, 0:8], axis=1, mode="promise_in_bounds")
    for i in range(3):
        for j in range(4):
            parts[4 * i + j] = upper[8 * i : 8 * i + 8, 128 * j : 128 * j + 128]
    for row in range(Q):
        i, k = divmod(WHERE[row] + 24, 8)
        for j in range(4):
            parts[4 * i + j, k : k + 1, :] = acc_out[row : row + 1, 128 * j : 128 * j + 128]
    for j in range(4):
        parts[28 + j, 7:8, :] = line[0:1] if j == 0 else jnp.zeros((1, 128), F32)

    def remote(src, dst, send, recv, to):
        return pltpu.make_async_remote_copy(
            src_ref=src, dst_ref=dst, send_sem=send, recv_sem=recv, device_id=to, device_id_type=MESH
        )

    mine = pl.multiple_of(core * 16, 16)
    other = pl.multiple_of((1 - core) * 16, 16)
    swap = remote(parts.at[pl.ds(other, 16)], from_core, core_send.at[0], core_recv.at[0], partner)
    swap.start()

    for pair in MIDDLE + OUTER:
        backward_field(pair)
    for half in range(2):
        for row in range(Q):
            by_q[0, WHERE[row], :, 128 * half : 128 * half + 128] = start[half, pl.ds(row, CZ, stride=ROWS), :]

    field_out = pltpu.make_async_copy(by_q, d_field, out_sem.at[0])
    field_out.start()
    swap.wait_recv()
    merged[...] = parts[pl.ds(mine, 16)] + from_core[...]
    per = 16 // ny
    scatter = []
    y_far_first = sorted(range(1, ny), key=lambda k: -min(k, ny - k))
    for k in y_far_first:
        piece = lax.rem(me_y + k, ny) * per
        scatter.append(remote(merged.at[pl.ds(piece, per)], from_y.at[k - 1], y_send.at[k - 1], y_recv.at[k - 1], at_y(k)))
    begin(scatter)
    end(scatter)
    total = merged[pl.ds(me_y * per, per)]
    for k in range(ny - 1):
        total = total + from_y[k]

    from_x[me_x] = total
    across = [
        remote(from_x.at[me_x], from_x.at[me_x], x_send.at[k - 1], x_recv.at[k - 1], at_x(k)) for k in range(1, nx)
    ]
    begin(across)
    end(across)
    total = from_x[0]
    for k in range(1, nx):
        total = total + from_x[k]

    from_z[me_z] = total
    far_first = sorted(range(1, nz), key=lambda k: -min(k, nz - k))
    along = [
        remote(from_z.at[me_z], from_z.at[me_z], z_send.at[k - 1], z_recv.at[k - 1], at_z(k)) for k in far_first
    ]
    begin(along)
    end(along)
    total = from_z[0]
    for k in range(1, nz):
        total = total + from_z[k]

    own = pl.ds(core * 16 + me_y * per, per)
    final[own] = total * scale
    def passed(k):
        return pl.ds(core * 16 + lax.rem(me_y + ny - k, ny) * per, per)

    spread_out = {
        k: remote(final.at[own], final.at[own], e_send.at[k - 1], e_recv.at[k - 1], at_y(k)) for k in y_far_first
    }
    begin(spread_out.values())
    give = {
        k: remote(final.at[passed(k)], final.at[passed(k)], g_send.at[k], g_recv.at[k], partner) for k in range(ny)
    }
    give[0].start()
    for k in sorted(range(1, ny), key=lambda k: min(k, ny - k)):
        spread_out[k].wait_recv()
        give[k].start()
    end(give.values())
    sums_out = pltpu.make_async_copy(final, sums, out_sem.at[1])
    sums_out.start()
    for copies in (copy_0, copy_1, copy_2, copy_3, copy_4, [swap], scatter, across, along, spread_out.values(), give.values()):
        for copy in copies:
            copy.wait_send()
    field_out.wait()
    sums_out.wait()


def write_out(field_at, sums_at, d_field, g_w_in, g_b_in, g_w_out, g_b_out, field, sums, a, b, c, d, sem):
    field_in = pltpu.make_async_copy(field_at, field, sem.at[0])
    sums_in = pltpu.make_async_copy(sums_at, sums, sem.at[1])
    sums_in.start()
    field_in.start()
    sums_in.wait()
    for j in range(4):
        cut = slice(128 * j, 128 * j + 128)
        a[0:8, cut] = sums[j]
        a[8:16, cut] = sums[4 + j]
        a[16:20, cut] = sums[8 + j, 0:4]
        b[:, cut] = sums[8 + j, 4:5]
        for i in range(3, 7):
            c[8 * i - 24 : 8 * i - 16, cut] = sums[4 * i + j]
        c[32:39, cut] = sums[28 + j, 0:7]
    d[...] = sums[28, 7:8, 0:Q]
    small = [
        pltpu.make_async_copy(src, dst, sem.at[i])
        for i, (src, dst) in enumerate([(a, g_w_in), (b, g_b_in), (c, g_w_out), (d, g_b_out)], 2)
    ]
    for copy in small:
        copy.start()
    field_in.wait()
    big = pltpu.make_async_copy(field, d_field, sem.at[6])
    big.start()
    for copy in small + [big]:
        copy.wait()


def solution(mesh):
    n_space, nx = mesh.shape["space"], mesh.shape["traj"]
    ny = 8 if n_space % 16 == 0 else 2
    nz = n_space // (2 * ny)
    scale = 1.0 / math.sqrt(float(n_space * nx * CELLS * STEPS))
    per = 16 // ny
    hbm = pl.BlockSpec(memory_space=pltpu.HBM)
    dma = pltpu.SemaphoreType.DMA

    def per_device(field, solid, cotangent, w_in, b_in, w_out, b_out):
        def body(*refs):
            kernel((ny, nz, nx), scale, *refs)

        d_field, sums = pl.pallas_call(
            body,
            out_shape=(jax.ShapeDtypeStruct(field.shape, F32), jax.ShapeDtypeStruct((32, 8, 128), F32)),
            in_specs=[hbm] * 9,
            out_specs=(hbm, hbm),
            scratch_shapes=[
                pltpu.VMEM(field.shape, F32),
                pltpu.VMEM(solid.shape, jnp.int32),
                pltpu.VMEM(field.shape, F32),
                pltpu.VMEM(w_in.shape, BF16),
                pltpu.VMEM((1, HID), F32),
                pltpu.VMEM((Q, HID), BF16),
                pltpu.VMEM((1, Q), F32),
                pltpu.VMEM(FLOATS.shape, F32),
                pltpu.VMEM(INTS.shape, jnp.int32),
                pltpu.VMEM(field.shape, F32),
                dma((9,)),
                dma((2,)),
                pltpu.VMEM((5, CZ + 6, ROWS, PLANE), F32),
                pltpu.VMEM((2, CZ * ROWS, 128), F32),
                pltpu.VMEM((2, CZ * ROWS, 128), F32),
                pltpu.VMEM((CZ, ROWS, PLANE), F32),
                pltpu.VMEM((CZ, ROWS, PLANE), F32),
                pltpu.VMEM((CZ, 8, PLANE), jnp.int32),
                pltpu.VMEM((STEPS, 128, CELLS), BF16),
                pltpu.VMEM((STEPS, HID, CELLS), BF16),
                pltpu.VMEM((HID, CELLS), BF16),
                pltpu.VMEM((HID, CELLS), BF16),
                pltpu.VMEM((48, CELLS), BF16),
                pltpu.VMEM((HID, 128), BF16),
                pltpu.VMEM((ROWS, HID), BF16),
                pltpu.VMEM((HID, 48), BF16),
                pltpu.VMEM((ROWS, HID), BF16),
                pltpu.VMEM((ROWS, PLANE), F32),
                pltpu.VMEM((128, HID), F32),
                pltpu.VMEM((48, HID), F32),
                pltpu.VMEM((ROWS, PLANE), F32),
                pltpu.VMEM((32, 8, 128), F32),
                pltpu.VMEM((16, 8, 128), F32),
                pltpu.VMEM((ny - 1, per, 8, 128), F32),
                pltpu.VMEM((nx, per, 8, 128), F32),
                pltpu.VMEM((nz, per, 8, 128), F32),
                pltpu.VMEM((16, 8, 128), F32),
                pltpu.VMEM((32, 8, 128), F32),
                dma((5, 4)), dma((5, 4)), dma((2,)), dma((2,)), dma((ny - 1,)), dma((ny - 1,)),
                dma((max(nx - 1, 1),)), dma((max(nx - 1, 1),)), dma((nz - 1,)), dma((nz - 1,)), dma((ny - 1,)), dma((ny - 1,)),
                dma((ny,)), dma((ny,)),
            ],
            compiler_params=pltpu.CompilerParams(collective_id=0, has_side_effects=True, vmem_limit_bytes=62 << 20),
            name="adjoint",
        )(field, solid, cotangent, w_in, b_in.reshape(1, HID), w_out.T, b_out.reshape(1, Q), jnp.asarray(FLOATS), jnp.asarray(INTS))
        d_field, g_w_in, g_b_in, g_w_out, g_b_out = pl.pallas_call(
            write_out,
            out_shape=(
                jax.ShapeDtypeStruct(field.shape, F32),
                jax.ShapeDtypeStruct((MOM, HID), F32),
                jax.ShapeDtypeStruct((1, HID), F32),
                jax.ShapeDtypeStruct((Q, HID), F32),
                jax.ShapeDtypeStruct((1, Q), F32),
            ),
            in_specs=[hbm, hbm],
            out_specs=(hbm,) * 5,
            scratch_shapes=[
                pltpu.VMEM(field.shape, F32), pltpu.VMEM((32, 8, 128), F32),
                pltpu.VMEM((MOM, HID), F32), pltpu.VMEM((1, HID), F32), pltpu.VMEM((Q, HID), F32), pltpu.VMEM((1, Q), F32),
                dma((7,)),
            ],
            compiler_params=pltpu.CompilerParams(vmem_limit_bytes=62 << 20),
            name="write_out",
        )(d_field, sums)
        return d_field, g_w_in, g_b_in.reshape(HID), g_w_out.T, g_b_out.reshape(Q)

    return jax.shard_map(
        per_device,
        mesh=mesh,
        in_specs=(P("traj", None, "space", None), P("traj", "space", None), P("traj", None, "space", None), P(), P(), P(), P()),
        out_specs=(P("traj", None, "space", None), P(), P(), P(), P()),
        check_vma=False,
    )
```

```python
import math

import jax
import jax.numpy as jnp
import numpy as np
from jax import lax
from jax.experimental import pallas as pl
from jax.experimental.pallas import tpu as pltpu
from jax.sharding import PartitionSpec as P

STEPS = 3
Q = 39
MOM = 20
HID = 512
CZ = 8
PLANE = 256
ROWS = 40
CELLS = CZ * PLANE
MESH = pl.DeviceIdType.MESH
F32 = jnp.float32
BF16 = jnp.bfloat16
NT = (((1,), (1,)), ((), ()))


def velocity_table():
    rows = [(0, 0, 0)]
    for axis_one in range(3):
        for sign in (1, -1):
            entry = [0, 0, 0]
            entry[axis_one] = sign
            rows.append(tuple(entry))
    for along_x in (1, -1):
        for along_y in (1, -1):
            for along_z in (1, -1):
                rows.append((along_x, along_y, along_z))
    for axis_one in range(3):
        for sign in (1, -1):
            entry = [0, 0, 0]
            entry[axis_one] = 2 * sign
            rows.append(tuple(entry))
    for first, second in ((0, 1), (0, 2), (1, 2)):
        for sign_one in (2, -2):
            for sign_two in (2, -2):
                entry = [0, 0, 0]
                entry[first] = sign_one
                entry[second] = sign_two
                rows.append(tuple(entry))
    for axis_one in range(3):
        for sign in (1, -1):
            entry = [0, 0, 0]
            entry[axis_one] = 3 * sign
            rows.append(tuple(entry))
    return rows


def hermite_table(velocity):
    sound = 2.0 / 3.0
    e = np.asarray(velocity, np.float64)
    ident = np.eye(3)
    rows = [np.ones(len(velocity))]
    for a in range(3):
        rows.append(e[:, a])
    for a in range(3):
        for b in range(a, 3):
            rows.append(e[:, a] * e[:, b] - sound * ident[a, b])
    for a in range(3):
        for b in range(a, 3):
            for c in range(b, 3):
                rows.append(
                    e[:, a] * e[:, b] * e[:, c]
                    - sound * (e[:, a] * ident[b, c] + e[:, b] * ident[a, c] + e[:, c] * ident[a, b])
                )
    return np.stack([r / np.sqrt((r * r).sum()) for r in rows]).astype(np.float32)


def row_order(velocity):
    up = [(0, 0, 3), (0, 0, 2), (2, 0, 2), (-2, 0, 2), (0, 2, 2), (0, -2, 2), (0, 0, 1), (1, 1, 1)]
    mixed = [(1, -1, 1), (-1, 1, 1), (-1, -1, 1), (1, 0, 0)]
    level = [(0, 1, 0), (2, 0, 0), (0, 2, 0), (2, 2, 0), (2, -2, 0), (3, 0, 0), (0, 3, 0)]
    neg = lambda group: [tuple(-v for v in e) for e in group]
    order = up + mixed + neg(mixed) + neg(up) + level + [(0, 0, 0)] + neg(level)
    assert sorted(order) == sorted(velocity)
    return order


def tables():
    velocity = velocity_table()
    order = row_order(velocity)
    where = [velocity.index(e) for e in order]
    herm = hermite_table(velocity)[:, where]
    herm = np.concatenate([herm, np.zeros((MOM, 1), np.float32)], axis=1)
    bf = lambda a: np.asarray(jnp.asarray(a).astype(BF16).astype(F32))
    hi = bf(herm)
    mid = bf(herm - hi)
    low = bf(herm - hi - mid)
    thick = np.concatenate([hi, mid, low, np.zeros((4, ROWS), np.float32)])
    spread = np.zeros((64, 128), np.float32)
    for part in range(3):
        spread[:, part * ROWS : (part + 1) * ROWS] = thick
    for part in range(3):
        spread[60 + part, 120 + part] = 1.0
    final = np.zeros((24, 128), np.float32)
    final[:MOM, :ROWS] = herm
    final[:MOM, ROWS : 2 * ROWS] = herm
    final[MOM, 120] = 1.0
    pick = np.zeros((48, 128), np.float32)
    for row, q in enumerate(where):
        pick[row, q] = 1.0
    floats = np.zeros((320, 128), np.float32)
    floats[0:64] = spread
    floats[64:88] = final
    floats[88:136] = pick
    floats[136:184, :48] = pick.T[:48, :48]
    floats[184:224, :64] = thick.T
    ints = np.zeros((5, ROWS, 128), np.int32)
    for row, q in enumerate(where):
        ints[4, :, q] = row
    for row, e in enumerate(order):
        for back, sign in ((0, 1), (1, -1)):
            for lane in range(128):
                x, y = lane // 16, lane % 16
                source = ((x - sign * e[0]) % 16) * 16 + (y - sign * e[1]) % 16
                ints[2 * back, row, lane] = source % 128
                ints[2 * back + 1, row, lane] = source // 128
    ints[0, 39], ints[2, 39] = np.arange(128), np.arange(128)
    ints[4, :, Q:] = ROWS - 1
    return where, floats, ints


WHERE, FLOATS, INTS = tables()


def kernel(
    grid, scale, *refs
):
    (
    field_at, solid_at, cotangent_at, w_in_at, b_in_at, w_out_at, b_out_at, floats_at, ints_at, d_field, sums,
    field, solid, cotangent, w_in, b_in, w_out, b_out, floats, ints, by_q, in_sem, out_sem, pads, start, back_in, state, bounce, walls, xs, hid, dact, dhs, gbs, w_stack, w_trans, wo, wo_trans, bias, acc_in, acc_out,
    acc_b, parts, from_core, from_xy, from_z, merged, final,
    halo_send, halo_recv, core_send, core_recv, xy_send, xy_recv, z_send, z_recv, e_send, e_recv, g_send, g_recv,
    ) = refs
    ny, nz, nx = grid
    me_s, me_x = lax.axis_index("space"), lax.axis_index("traj")
    core = lax.rem(me_s, 2)
    me_z = lax.rem(me_s // 2, nz)
    me_y = me_s // (2 * nz)
    n_space = ny * nz * 2
    up = (lax.rem(me_s + 1, n_space), me_x)
    down = (lax.rem(me_s + n_space - 1, n_space), me_x)
    place = lambda y, z, c: (y * nz + z) * 2 + c
    partner = (place(me_y, me_z, 1 - core), me_x)
    at = lambda dy, dx: (place(lax.rem(me_y + dy, ny), me_z, core), lax.rem(me_x + dx, nx))
    at_z = lambda k: (place(me_y, lax.rem(me_z + k, nz), core), me_x)
    hops = lambda k, n: min(k, n - k)
    others = [(dy, dx) for dy in range(ny) for dx in range(nx) if dy or dx]
    others.sort(key=lambda d: -hops(d[0], ny) - hops(d[1], nx))
    peers = [up, down] + [at(*d) for d in others] + [at_z(k) for k in range(1, nz)]

    copies_in = [
        pltpu.make_async_copy(src, dst, in_sem.at[i])
        for i, (src, dst) in enumerate(
            [
                (floats_at, floats), (w_in_at, w_in), (b_in_at, b_in), (w_out_at, w_out), (b_out_at, b_out),
                (field_at, field), (solid_at, solid), (ints_at, ints), (cotangent_at, cotangent),
            ]
        )
    ]
    for copy in copies_in:
        copy.start()
    barrier = pltpu.get_barrier_semaphore()
    for peer in peers:
        pl.semaphore_signal(barrier, inc=1, device_id=peer, device_id_type=MESH)

    for copy in copies_in[:5]:
        copy.wait()

    w = w_in[...].astype(F32)
    b = b_in[...]
    b_hi = b.astype(BF16).astype(F32)
    b_mid = (b - b_hi).astype(BF16).astype(F32)
    b_low = b - b_hi - b_mid
    stack = jnp.concatenate([w, w, w, b_hi, b_mid, b_low, jnp.zeros((1, HID), F32)], axis=0)
    spread = floats[0:64, :].astype(BF16)
    full = jnp.dot(stack.T.astype(BF16), spread, preferred_element_type=F32)
    column = lax.broadcasted_iota(jnp.int32, (HID, 128), 1)
    low_part = full - full.astype(BF16).astype(F32)
    w_stack[...] = jnp.where((column >= 2 * ROWS) & (column < 3 * ROWS), low_part, full).astype(BF16)
    thick_t = floats[184:224, 0:64].astype(BF16)
    w_trans[...] = jnp.dot(thick_t, stack.astype(BF16), preferred_element_type=F32).astype(BF16)
    pick = floats[88:136, 0:Q].astype(BF16)
    by_row = jnp.dot(pick, w_out[...], preferred_element_type=F32)
    wo[...] = by_row.T.astype(BF16)
    wo_trans[...] = by_row[:ROWS].astype(BF16)
    bo = lax.dot_general(
        floats[88:136, 0:Q], jnp.broadcast_to(b_out[...], (8, Q)), NT, precision=lax.Precision.HIGHEST, preferred_element_type=F32
    )
    bias[...] = jnp.broadcast_to(bo[:ROWS, 0:1], (ROWS, PLANE))
    acc_b[...] = jnp.zeros((ROWS, PLANE), F32)

    zeros = jnp.zeros((CZ, 128), F32)

    def by_plane(source, rows):
        for half in range(2):
            lanes = slice(128 * half, 128 * half + 128)
            for row in range(ROWS):
                value = source[0, WHERE[row], :, lanes] if row < Q else zeros
                rows[half, pl.ds(row, CZ, stride=ROWS), :] = value

    copies_in[5].wait()
    by_plane(field, start)

    row8 = lax.broadcasted_iota(jnp.int32, (8, PLANE), 0)

    def wall_of(z):
        return walls[z] > 0

    def opposite(v):
        last = row8 == 7
        return jnp.concatenate(
            [
                v[16:24],
                jnp.concatenate([v[12:16], v[8:12]], axis=0),
                v[0:8],
                jnp.where(last, v[24:32], v[32:40]),
                jnp.where(last, v[32:40], v[24:32]),
            ],
            axis=0,
        )

    def select(wall, a, b):
        return jnp.concatenate([jnp.where(wall, a[8 * i : 8 * i + 8], b[8 * i : 8 * i + 8]) for i in range(5)], axis=0)

    def streamed(pad, z, sign):
        here = z + 3
        plane = lambda by, rows: pad[here - sign * by, rows, :]
        a, m, o, r = slice(0, 8), slice(8, 16), slice(16, 24), slice(24, 40)
        top = jnp.where(row8 == 0, plane(3, a), jnp.where(row8 < 6, plane(2, a), plane(1, a)))
        mix = jnp.where(row8 < 3, plane(1, m), jnp.where((row8 > 3) & (row8 < 7), plane(-1, m), plane(0, m)))
        low = jnp.where(row8 == 0, plane(-3, o), jnp.where(row8 < 6, plane(-2, o), plane(-1, o)))
        v = jnp.concatenate([top, mix, low, plane(0, r)], axis=0)
        which = 0 if sign == 1 else 2
        index, far = ints[which], ints[which + 1] > 0
        left = jnp.take_along_axis(v[:, 0:128], index, axis=1, mode="promise_in_bounds")
        right = jnp.take_along_axis(v[:, 128:256], index, axis=1, mode="promise_in_bounds")
        return jnp.concatenate([jnp.where(far, right, left), jnp.where(far, left, right)], axis=1)

    def cells_of(z):
        return slice(z * PLANE, z * PLANE + PLANE)

    def loaded(ref, z):
        rows = slice(z * ROWS, z * ROWS + ROWS)
        return jnp.concatenate([ref[0, rows, :], ref[1, rows, :]], axis=1)

    ones = jnp.ones((8, 2 * PLANE), F32)

    def side_by_side(parts):
        return jnp.concatenate(parts, axis=1)

    def forward_hidden(t, pair):
        values = []
        for z in pair:
            if t == 0:
                values.append(loaded(start, z))
            else:
                pad = pads.at[t]
                values.append(select(wall_of(z), opposite(pad[z + 3]), streamed(pad, z, 1)))
        v = side_by_side(values)
        v_hi = v.astype(BF16).astype(F32)
        x = jnp.concatenate([v_hi, v - v_hi, v_hi, ones], axis=0).astype(BF16)
        for i, z in enumerate(pair):
            xs[t, :, cells_of(z)] = x[:, PLANE * i : PLANE * i + PLANE]
        halves = []
        for c in range(2):
            rows = slice(256 * c, 256 * c + 256)
            act = jnp.dot(w_stack[rows, :], x, preferred_element_type=F32)
            wide = jnp.tanh(act)
            h = wide.astype(BF16)
            for i, z in enumerate(pair):
                hid[t, rows, cells_of(z)] = h[:, PLANE * i : PLANE * i + PLANE]
            if t == 2:
                wide = h.astype(F32)
                dh = side_by_side([dhs[rows, cells_of(z)] for z in pair]).astype(F32)
                h = (dh * (1.0 - wide * wide)).astype(BF16)
                for i, z in enumerate(pair):
                    dact[rows, cells_of(z)] = h[:, PLANE * i : PLANE * i + PLANE]
            halves.append(h)
        return v, jnp.concatenate(halves, axis=0)

    def forward_change(t, pair, done):
        if t == 2:
            g = side_by_side([state[z] for z in pair])
            backward_change(2, pair, (g, done[1]))
        else:
            v, h = done
            change = jnp.dot(wo_trans[...], h, preferred_element_type=F32)
            for i, z in enumerate(pair):
                cut = slice(PLANE * i, PLANE * i + PLANE)
                pads[t + 1, z + 3] = v[:, cut] + change[:, cut] + bias[...]

    def outgoing(z, g, slot):
        wall = wall_of(z)
        nothing = jnp.zeros((ROWS, PLANE), F32)
        bounce[z] = select(wall, opposite(g), nothing)
        pads[slot, z + 3] = select(wall, nothing, g)

    def backward_post(t, pair):
        slot = (4, 3, 0)[t]
        posts = [streamed(pads.at[slot], z, -1) + bounce[z] for z in pair]
        acc_b[...] += posts[0] + posts[1]
        g_post = side_by_side(posts)
        gb = jnp.concatenate([g_post, jnp.zeros((8, 2 * PLANE), F32)], axis=0).astype(BF16)
        for i, z in enumerate(pair):
            gbs[:, cells_of(z)] = gb[:, PLANE * i : PLANE * i + PLANE]
            if t != 1:
                state[z] = posts[i]
        return g_post, gb

    def backward_ahead(pair):
        g_post, gb = backward_post(2, pair)
        for c in range(2):
            rows = slice(256 * c, 256 * c + 256)
            dh = jnp.dot(wo[rows, :], gb, preferred_element_type=F32).astype(BF16)
            for i, z in enumerate(pair):
                dhs[rows, cells_of(z)] = dh[:, PLANE * i : PLANE * i + PLANE]

    def backward_hidden(t, pair):
        g_post, gb = backward_post(t, pair)
        halves = []
        for c in range(2):
            rows = slice(256 * c, 256 * c + 256)
            dh = jnp.dot(wo[rows, :], gb, preferred_element_type=F32)
            h = side_by_side([hid[t, rows, cells_of(z)] for z in pair]).astype(F32)
            da = (dh * (1.0 - h * h)).astype(BF16)
            for i, z in enumerate(pair):
                dact[rows, cells_of(z)] = da[:, PLANE * i : PLANE * i + PLANE]
            halves.append(da)
        return g_post, jnp.concatenate(halves, axis=0)

    def backward_field(pair):
        da = side_by_side([dact[:, cells_of(z)] for z in pair])
        change = jnp.dot(w_trans[...], da, preferred_element_type=F32)
        for i, z in enumerate(pair):
            g = state[z] + change[:, PLANE * i : PLANE * i + PLANE]
            for half in range(2):
                start[half, ROWS * z : ROWS * z + ROWS, :] = g[:, 128 * half : 128 * half + 128]

    def backward_change(t, pair, done):
        g_post, da = done
        g = g_post + jnp.dot(w_trans[...], da, preferred_element_type=F32)
        for i, z in enumerate(pair):
            cut = slice(PLANE * i, PLANE * i + PLANE)
            outgoing(z, g[:, cut], 5 - t)

    def grads(t):
        g_in = lax.dot_general(xs[t], dact[...], NT, preferred_element_type=F32)
        g_out = lax.dot_general(gbs[...], hid[t], NT, preferred_element_type=F32)
        if t == 2:
            acc_in[...] = g_in
            acc_out[...] = g_out
        else:
            acc_in[...] += g_in
            acc_out[...] += g_out

    def halo(slot, sign):
        first, second = (up, down) if sign == 1 else (down, up)
        pad = pads.at[slot]
        if sign == 1:
            moves = [
                (pad.at[10, 0:16], pad.at[2, 0:16], up),
                (pad.at[8:10, 0:8], pad.at[0:2, 0:8], up),
                (pad.at[3, 8:24], pad.at[11, 8:24], down),
                (pad.at[4:6, 16:24], pad.at[12:14, 16:24], down),
            ]
        else:
            moves = [
                (pad.at[3, 0:16], pad.at[11, 0:16], down),
                (pad.at[4:6, 0:8], pad.at[12:14, 0:8], down),
                (pad.at[10, 8:24], pad.at[2, 8:24], up),
                (pad.at[8:10, 16:24], pad.at[0:2, 16:24], up),
            ]
        return [
            pltpu.make_async_remote_copy(
                src_ref=src, dst_ref=dst, send_sem=halo_send.at[slot, i], recv_sem=halo_recv.at[slot, i],
                device_id=to, device_id_type=MESH,
            )
            for i, (src, dst, to) in enumerate(moves)
        ]

    def begin(copies):
        for copy in copies:
            copy.start()

    def end(copies):
        for copy in copies:
            copy.wait_recv()

    MIDDLE, OUTER = [(3, 4)], [(0, 1), (2, 5), (6, 7)]

    def in_turn(first, second, t, pairs, before=None):
        done = None
        for pair in pairs:
            if before is not None and pair in OUTER:
                end(before)
                before = None
            now = first(t, pair)
            if done is not None:
                second(t, *done)
            done = (pair, now)
        second(t, *done)

    def forwards(t, pairs, before=None):
        in_turn(forward_hidden, forward_change, t, pairs, before)

    def nothing(t, pair, done):
        pass

    forwards(0, OUTER)
    for copy in copies_in[6:8]:
        copy.wait()
    pl.semaphore_wait(barrier, len(peers))
    copy_1 = halo(1, 1)
    begin(copy_1)
    for z in range(CZ):
        walls[z] = jnp.broadcast_to(solid[0, z : z + 1, :], (8, PLANE))
    copies_in[8].wait()
    by_plane(cotangent, back_in)
    for z in range(CZ):
        outgoing(z, loaded(back_in, z), 0)
    copy_0 = halo(0, -1)
    begin(copy_0)
    forwards(0, MIDDLE)
    forwards(1, MIDDLE + OUTER, copy_1)
    copy_2 = halo(2, 1)
    begin(copy_2)
    end(copy_0)
    for pair in MIDDLE + OUTER:
        backward_ahead(pair)
    end(copy_2)
    forwards(2, OUTER)
    copy_3 = halo(3, -1)
    begin(copy_3)
    forwards(2, MIDDLE)
    grads(2)
    in_turn(backward_hidden, backward_change, 1, MIDDLE + OUTER, copy_3)
    copy_4 = halo(4, -1)
    begin(copy_4)
    grads(1)
    in_turn(backward_hidden, nothing, 0, MIDDLE + OUTER, copy_4)
    grads(0)

    def two(v):
        v_hi = v.astype(BF16).astype(F32)
        return v_hi, v - v_hi

    a_hi, a_low = two(acc_in[...])
    f_hi, f_low = two(floats[64:88, :])
    left = jnp.concatenate([f_hi, f_hi], axis=1).astype(BF16)
    right = jnp.concatenate([a_hi, a_low], axis=0).astype(BF16)
    upper = jnp.dot(left, right, preferred_element_type=F32)
    upper = upper + jnp.dot(f_low.astype(BF16), a_hi.astype(BF16), preferred_element_type=F32)
    b_hi, b_low = two(acc_b[...])
    pair = jnp.concatenate([b_hi, jnp.zeros((24, PLANE), F32), b_low, jnp.zeros((24, PLANE), F32)], axis=0).astype(BF16)
    line = lax.dot_general(jnp.ones((8, PLANE), BF16), pair, NT, preferred_element_type=F32)
    line = line + jnp.concatenate([line[:, 64:], line[:, :64]], axis=1)
    line = jnp.take_along_axis(line, ints[4, 0:8], axis=1, mode="promise_in_bounds")
    parts[MOM + 1 : 24] = jnp.zeros((23 - MOM, 4, 128), F32)
    for j in range(4):
        cut = slice(128 * j, 128 * j + 128)
        for row in range(MOM + 1):
            parts[row, j : j + 1, :] = upper[row : row + 1, cut]
        for row in range(Q):
            parts[24 + WHERE[row], j : j + 1, :] = acc_out[row : row + 1, cut]
        parts[63, j : j + 1, :] = line[0:1] if j == 0 else jnp.zeros((1, 128), F32)

    def remote(src, dst, send, recv, to):
        return pltpu.make_async_remote_copy(
            src_ref=src, dst_ref=dst, send_sem=send, recv_sem=recv, device_id=to, device_id_type=MESH
        )

    mine = core * 32
    other = 32 - mine
    swap = remote(parts.at[pl.ds(other, 32)], from_core, core_send.at[0], core_recv.at[0], partner)
    swap.start()

    for pair in MIDDLE + OUTER:
        backward_field(pair)
    for half in range(2):
        for row in range(Q):
            by_q[0, WHERE[row], :, 128 * half : 128 * half + 128] = start[half, pl.ds(row, CZ, stride=ROWS), :]

    field_out = pltpu.make_async_copy(by_q, d_field, out_sem.at[0])
    field_out.start()
    swap.wait_recv()
    merged[...] = parts[pl.ds(mine, 32)] + from_core[...]
    per = 32 // (ny * nx)
    share = lambda dy, dx: (lax.rem(me_y + dy, ny) * nx + lax.rem(me_x + dx, nx)) * per
    scatter = []
    for i, (dy, dx) in enumerate(others):
        src = merged.at[pl.ds(share(dy, dx), per)]
        scatter.append(remote(src, from_xy.at[i], xy_send.at[i], xy_recv.at[i], at(dy, dx)))
    begin(scatter)
    end(scatter)
    total = merged[pl.ds(share(0, 0), per)]
    for i in range(len(others)):
        total = total + from_xy[i]

    from_z[me_z] = total
    far_first = sorted(range(1, nz), key=lambda k: -min(k, nz - k))
    along = [
        remote(from_z.at[me_z], from_z.at[me_z], z_send.at[k - 1], z_recv.at[k - 1], at_z(k)) for k in far_first
    ]
    begin(along)
    end(along)
    total = from_z[0]
    for k in range(1, nz):
        total = total + from_z[k]

    own = pl.ds(mine + share(0, 0), per)
    final[own] = total * scale
    spread_out = [
        remote(final.at[own], final.at[own], e_send.at[i], e_recv.at[i], at(dy, dx)) for i, (dy, dx) in enumerate(others)
    ]
    begin(spread_out)
    give = []
    for k in sorted(range(ny), key=lambda k: hops(k, ny)):
        for i, (dy, dx) in enumerate(others):
            if dy == k:
                spread_out[i].wait_recv()
        line_of_x = final.at[pl.ds(mine + lax.rem(me_y + ny - k, ny) * nx * per, nx * per)]
        give.append(remote(line_of_x, line_of_x, g_send.at[k], g_recv.at[k], partner))
        give[-1].start()
    end(give)
    sums_out = pltpu.make_async_copy(final, sums, out_sem.at[1])
    sums_out.start()
    for copies in (copy_0, copy_1, copy_2, copy_3, copy_4, [swap], scatter, along, spread_out, give):
        for copy in copies:
            copy.wait_send()
    field_out.wait()
    sums_out.wait()


def write_out(field_at, sums_at, d_field, g_w_in, g_b_in, g_w_out, g_b_out, field, sums, a, b, c, d, sem):
    field_in = pltpu.make_async_copy(field_at, field, sem.at[0])
    sums_in = pltpu.make_async_copy(sums_at, sums, sem.at[1])
    sums_in.start()
    field_in.start()
    sums_in.wait()
    for j in range(4):
        cut = slice(128 * j, 128 * j + 128)
        for row in range(MOM):
            a[row : row + 1, cut] = sums[row, j : j + 1, :]
        b[:, cut] = sums[MOM, j : j + 1, :]
        for row in range(Q):
            c[row : row + 1, cut] = sums[24 + row, j : j + 1, :]
    d[...] = sums[63, 0:1, 0:Q]
    small = [
        pltpu.make_async_copy(src, dst, sem.at[i])
        for i, (src, dst) in enumerate([(a, g_w_in), (b, g_b_in), (c, g_w_out), (d, g_b_out)], 2)
    ]
    for copy in small:
        copy.start()
    field_in.wait()
    big = pltpu.make_async_copy(field, d_field, sem.at[6])
    big.start()
    for copy in small + [big]:
        copy.wait()


def solution(mesh):
    n_space, nx = mesh.shape["space"], mesh.shape["traj"]
    ny = 8 if n_space % 16 == 0 else 2
    nz = n_space // (2 * ny)
    scale = 1.0 / math.sqrt(float(n_space * nx * CELLS * STEPS))
    per = 32 // (ny * nx)
    hbm = pl.BlockSpec(memory_space=pltpu.HBM)
    dma = pltpu.SemaphoreType.DMA

    def per_device(field, solid, cotangent, w_in, b_in, w_out, b_out):
        def body(*refs):
            kernel((ny, nz, nx), scale, *refs)

        d_field, sums = pl.pallas_call(
            body,
            out_shape=(jax.ShapeDtypeStruct(field.shape, F32), jax.ShapeDtypeStruct((64, 4, 128), F32)),
            in_specs=[hbm] * 9,
            out_specs=(hbm, hbm),
            scratch_shapes=[
                pltpu.VMEM(field.shape, F32),
                pltpu.VMEM(solid.shape, jnp.int32),
                pltpu.VMEM(field.shape, F32),
                pltpu.VMEM(w_in.shape, BF16),
                pltpu.VMEM((1, HID), F32),
                pltpu.VMEM((Q, HID), BF16),
                pltpu.VMEM((1, Q), F32),
                pltpu.VMEM(FLOATS.shape, F32),
                pltpu.VMEM(INTS.shape, jnp.int32),
                pltpu.VMEM(field.shape, F32),
                dma((9,)),
                dma((2,)),
                pltpu.VMEM((5, CZ + 6, ROWS, PLANE), F32),
                pltpu.VMEM((2, CZ * ROWS, 128), F32),
                pltpu.VMEM((2, CZ * ROWS, 128), F32),
                pltpu.VMEM((CZ, ROWS, PLANE), F32),
                pltpu.VMEM((CZ, ROWS, PLANE), F32),
                pltpu.VMEM((CZ, 8, PLANE), jnp.int32),
                pltpu.VMEM((STEPS, 128, CELLS), BF16),
                pltpu.VMEM((STEPS, HID, CELLS), BF16),
                pltpu.VMEM((HID, CELLS), BF16),
                pltpu.VMEM((HID, CELLS), BF16),
                pltpu.VMEM((48, CELLS), BF16),
                pltpu.VMEM((HID, 128), BF16),
                pltpu.VMEM((ROWS, HID), BF16),
                pltpu.VMEM((HID, 48), BF16),
                pltpu.VMEM((ROWS, HID), BF16),
                pltpu.VMEM((ROWS, PLANE), F32),
                pltpu.VMEM((128, HID), F32),
                pltpu.VMEM((48, HID), F32),
                pltpu.VMEM((ROWS, PLANE), F32),
                pltpu.VMEM((64, 4, 128), F32),
                pltpu.VMEM((32, 4, 128), F32),
                pltpu.VMEM((ny * nx - 1, per, 4, 128), F32),
                pltpu.VMEM((nz, per, 4, 128), F32),
                pltpu.VMEM((32, 4, 128), F32),
                pltpu.VMEM((64, 4, 128), F32),
                dma((5, 4)), dma((5, 4)), dma((2,)), dma((2,)), dma((ny * nx - 1,)), dma((ny * nx - 1,)),
                dma((nz - 1,)), dma((nz - 1,)), dma((ny * nx - 1,)), dma((ny * nx - 1,)), dma((ny,)), dma((ny,)),
            ],
            compiler_params=pltpu.CompilerParams(collective_id=0, has_side_effects=True, vmem_limit_bytes=62 << 20),
            name="adjoint",
        )(field, solid, cotangent, w_in, b_in.reshape(1, HID), w_out.T, b_out.reshape(1, Q), jnp.asarray(FLOATS), jnp.asarray(INTS))
        d_field, g_w_in, g_b_in, g_w_out, g_b_out = pl.pallas_call(
            write_out,
            out_shape=(
                jax.ShapeDtypeStruct(field.shape, F32),
                jax.ShapeDtypeStruct((MOM, HID), F32),
                jax.ShapeDtypeStruct((1, HID), F32),
                jax.ShapeDtypeStruct((Q, HID), F32),
                jax.ShapeDtypeStruct((1, Q), F32),
            ),
            in_specs=[hbm, hbm],
            out_specs=(hbm,) * 5,
            scratch_shapes=[
                pltpu.VMEM(field.shape, F32), pltpu.VMEM((64, 4, 128), F32),
                pltpu.VMEM((MOM, HID), F32), pltpu.VMEM((1, HID), F32), pltpu.VMEM((Q, HID), F32), pltpu.VMEM((1, Q), F32),
                dma((7,)),
            ],
            compiler_params=pltpu.CompilerParams(vmem_limit_bytes=62 << 20),
            name="write_out",
        )(d_field, sums)
        return d_field, g_w_in, g_b_in.reshape(HID), g_w_out.T, g_b_out.reshape(Q)

    return jax.shard_map(
        per_device,
        mesh=mesh,
        in_specs=(P("traj", None, "space", None), P("traj", "space", None), P("traj", None, "space", None), P(), P(), P(), P()),
        out_specs=(P("traj", None, "space", None), P(), P(), P(), P()),
        check_vma=False,
    )
```

```python
import math

import jax
import jax.numpy as jnp
import numpy as np
from jax import lax
from jax.experimental import pallas as pl
from jax.experimental.pallas import tpu as pltpu
from jax.sharding import PartitionSpec as P

STEPS = 3
Q = 39
MOM = 20
HID = 512
CZ = 8
PLANE = 256
ROWS = 40
CELLS = CZ * PLANE
MESH = pl.DeviceIdType.MESH
F32 = jnp.float32
BF16 = jnp.bfloat16
NT = (((1,), (1,)), ((), ()))


def velocity_table():
    rows = [(0, 0, 0)]
    for axis_one in range(3):
        for sign in (1, -1):
            entry = [0, 0, 0]
            entry[axis_one] = sign
            rows.append(tuple(entry))
    for along_x in (1, -1):
        for along_y in (1, -1):
            for along_z in (1, -1):
                rows.append((along_x, along_y, along_z))
    for axis_one in range(3):
        for sign in (1, -1):
            entry = [0, 0, 0]
            entry[axis_one] = 2 * sign
            rows.append(tuple(entry))
    for first, second in ((0, 1), (0, 2), (1, 2)):
        for sign_one in (2, -2):
            for sign_two in (2, -2):
                entry = [0, 0, 0]
                entry[first] = sign_one
                entry[second] = sign_two
                rows.append(tuple(entry))
    for axis_one in range(3):
        for sign in (1, -1):
            entry = [0, 0, 0]
            entry[axis_one] = 3 * sign
            rows.append(tuple(entry))
    return rows


def hermite_table(velocity):
    sound = 2.0 / 3.0
    e = np.asarray(velocity, np.float64)
    ident = np.eye(3)
    rows = [np.ones(len(velocity))]
    for a in range(3):
        rows.append(e[:, a])
    for a in range(3):
        for b in range(a, 3):
            rows.append(e[:, a] * e[:, b] - sound * ident[a, b])
    for a in range(3):
        for b in range(a, 3):
            for c in range(b, 3):
                rows.append(
                    e[:, a] * e[:, b] * e[:, c]
                    - sound * (e[:, a] * ident[b, c] + e[:, b] * ident[a, c] + e[:, c] * ident[a, b])
                )
    return np.stack([r / np.sqrt((r * r).sum()) for r in rows]).astype(np.float32)


def row_order(velocity):
    up = [(0, 0, 3), (0, 0, 2), (2, 0, 2), (-2, 0, 2), (0, 2, 2), (0, -2, 2), (0, 0, 1), (1, 1, 1)]
    mixed = [(1, -1, 1), (-1, 1, 1), (-1, -1, 1), (1, 0, 0)]
    level = [(0, 1, 0), (2, 0, 0), (0, 2, 0), (2, 2, 0), (2, -2, 0), (3, 0, 0), (0, 3, 0)]
    neg = lambda group: [tuple(-v for v in e) for e in group]
    order = up + mixed + neg(mixed) + neg(up) + level + [(0, 0, 0)] + neg(level)
    assert sorted(order) == sorted(velocity)
    return order


def tables():
    velocity = velocity_table()
    order = row_order(velocity)
    where = [velocity.index(e) for e in order]
    herm = hermite_table(velocity)[:, where]
    herm = np.concatenate([herm, np.zeros((MOM, 1), np.float32)], axis=1)
    bf = lambda a: np.asarray(jnp.asarray(a).astype(BF16).astype(F32))
    hi = bf(herm)
    mid = bf(herm - hi)
    low = bf(herm - hi - mid)
    thick = np.concatenate([hi, mid, low, np.zeros((4, ROWS), np.float32)])
    spread = np.zeros((64, 128), np.float32)
    for part in range(3):
        spread[:, part * ROWS : (part + 1) * ROWS] = thick
    for part in range(3):
        spread[60 + part, 120 + part] = 1.0
    final = np.zeros((24, 128), np.float32)
    final[:MOM, :ROWS] = herm
    final[:MOM, ROWS : 2 * ROWS] = herm
    final[MOM, 120] = 1.0
    pick = np.zeros((48, 128), np.float32)
    for row, q in enumerate(where):
        pick[row, q] = 1.0
    floats = np.zeros((320, 128), np.float32)
    floats[0:64] = spread
    floats[64:88] = final
    floats[88:136] = pick
    floats[136:184, :48] = pick.T[:48, :48]
    floats[184:224, :64] = thick.T
    ints = np.zeros((5, ROWS, 128), np.int32)
    for row, q in enumerate(where):
        ints[4, :, q] = row
    for row, e in enumerate(order):
        for back, sign in ((0, 1), (1, -1)):
            for lane in range(128):
                x, y = lane // 16, lane % 16
                source = ((x - sign * e[0]) % 16) * 16 + (y - sign * e[1]) % 16
                ints[2 * back, row, lane] = source % 128
                ints[2 * back + 1, row, lane] = source // 128
    ints[0, 39], ints[2, 39] = np.arange(128), np.arange(128)
    ints[4, :, Q:] = ROWS - 1
    return where, floats, ints


WHERE, FLOATS, INTS = tables()


def kernel(
    grid, scale, *refs
):
    (
    field_at, solid_at, cotangent_at, w_in_at, b_in_at, w_out_at, b_out_at, floats_at, ints_at, d_field, sums,
    field, solid, cotangent, w_in, b_in, w_out, b_out, floats, ints, by_q, in_sem, out_sem, pads, start, back_in, state, bounce, walls, xs, hid, dact, dhs, gbs, w_stack, w_trans, wo, wo_trans, bias, acc_in, acc_out,
    acc_b, parts, from_core, from_xy, from_z, merged, final,
    halo_send, halo_recv, core_send, core_recv, xy_send, xy_recv, z_send, z_recv, e_send, e_recv, g_send, g_recv,
    ) = refs
    ny, nz, nx = grid
    me_s, me_x = lax.axis_index("space"), lax.axis_index("traj")
    core = lax.rem(me_s, 2)
    me_z = lax.rem(me_s // 2, nz)
    me_y = me_s // (2 * nz)
    n_space = ny * nz * 2
    up = (lax.rem(me_s + 1, n_space), me_x)
    down = (lax.rem(me_s + n_space - 1, n_space), me_x)
    place = lambda y, z, c: (y * nz + z) * 2 + c
    partner = (place(me_y, me_z, 1 - core), me_x)
    at = lambda dy, dx: (place(lax.rem(me_y + dy, ny), me_z, core), lax.rem(me_x + dx, nx))
    at_z = lambda k: (place(me_y, lax.rem(me_z + k, nz), core), me_x)
    hops = lambda k, n: min(k, n - k)
    others = [(dy, dx) for dy in range(ny) for dx in range(nx) if dy or dx]
    others.sort(key=lambda d: -hops(d[0], ny) - hops(d[1], nx))
    peers = [up, down] + [at(*d) for d in others] + [at_z(k) for k in range(1, nz)]

    copies_in = [
        pltpu.make_async_copy(src, dst, in_sem.at[i])
        for i, (src, dst) in enumerate(
            [
                (floats_at, floats), (w_in_at, w_in), (b_in_at, b_in), (w_out_at, w_out), (b_out_at, b_out),
                (field_at, field), (solid_at, solid), (ints_at, ints), (cotangent_at, cotangent),
            ]
        )
    ]
    for copy in copies_in:
        copy.start()
    barrier = pltpu.get_barrier_semaphore()
    for peer in peers:
        pl.semaphore_signal(barrier, inc=1, device_id=peer, device_id_type=MESH)

    for copy in copies_in[:5]:
        copy.wait()

    w = w_in[...].astype(F32)
    b = b_in[...]
    b_hi = b.astype(BF16).astype(F32)
    b_mid = (b - b_hi).astype(BF16).astype(F32)
    b_low = b - b_hi - b_mid
    stack = jnp.concatenate([w, w, w, b_hi, b_mid, b_low, jnp.zeros((1, HID), F32)], axis=0)
    spread = floats[0:64, :].astype(BF16)
    full = jnp.dot(stack.T.astype(BF16), spread, preferred_element_type=F32)
    column = lax.broadcasted_iota(jnp.int32, (HID, 128), 1)
    low_part = full - full.astype(BF16).astype(F32)
    w_stack[...] = jnp.where((column >= 2 * ROWS) & (column < 3 * ROWS), low_part, full).astype(BF16)
    pick = floats[88:136, 0:Q].astype(BF16)
    by_row = jnp.dot(pick, w_out[...], preferred_element_type=F32)
    wo_trans[...] = by_row[:ROWS].astype(BF16)
    bo = lax.dot_general(
        floats[88:136, 0:Q], jnp.broadcast_to(b_out[...], (8, Q)), NT, precision=lax.Precision.HIGHEST, preferred_element_type=F32
    )
    bias[...] = jnp.broadcast_to(bo[:ROWS, 0:1], (ROWS, PLANE))

    zeros = jnp.zeros((CZ, 128), F32)

    def by_plane(source, rows):
        for half in range(2):
            lanes = slice(128 * half, 128 * half + 128)
            for row in range(ROWS):
                value = source[0, WHERE[row], :, lanes] if row < Q else zeros
                rows[half, pl.ds(row, CZ, stride=ROWS), :] = value

    copies_in[5].wait()
    by_plane(field, start)

    row8 = lax.broadcasted_iota(jnp.int32, (8, PLANE), 0)

    def wall_of(z):
        return walls[z] > 0

    def opposite(v):
        last = row8 == 7
        return jnp.concatenate(
            [
                v[16:24],
                jnp.concatenate([v[12:16], v[8:12]], axis=0),
                v[0:8],
                jnp.where(last, v[24:32], v[32:40]),
                jnp.where(last, v[32:40], v[24:32]),
            ],
            axis=0,
        )

    def select(wall, a, b):
        return jnp.concatenate([jnp.where(wall, a[8 * i : 8 * i + 8], b[8 * i : 8 * i + 8]) for i in range(5)], axis=0)

    def streamed(pad, z, sign):
        here = z + 3
        plane = lambda by, rows: pad[here - sign * by, rows, :]
        a, m, o, r = slice(0, 8), slice(8, 16), slice(16, 24), slice(24, 40)
        top = jnp.where(row8 == 0, plane(3, a), jnp.where(row8 < 6, plane(2, a), plane(1, a)))
        mix = jnp.where(row8 < 3, plane(1, m), jnp.where((row8 > 3) & (row8 < 7), plane(-1, m), plane(0, m)))
        low = jnp.where(row8 == 0, plane(-3, o), jnp.where(row8 < 6, plane(-2, o), plane(-1, o)))
        v = jnp.concatenate([top, mix, low, plane(0, r)], axis=0)
        which = 0 if sign == 1 else 2
        index, far = ints[which], ints[which + 1] > 0
        left = jnp.take_along_axis(v[:, 0:128], index, axis=1, mode="promise_in_bounds")
        right = jnp.take_along_axis(v[:, 128:256], index, axis=1, mode="promise_in_bounds")
        return jnp.concatenate([jnp.where(far, right, left), jnp.where(far, left, right)], axis=1)

    def cells_of(z):
        return slice(z * PLANE, z * PLANE + PLANE)

    def loaded(ref, z):
        rows = slice(z * ROWS, z * ROWS + ROWS)
        return jnp.concatenate([ref[0, rows, :], ref[1, rows, :]], axis=1)

    ones = jnp.ones((8, 2 * PLANE), F32)

    def side_by_side(parts):
        return jnp.concatenate(parts, axis=1)

    def forward_hidden(t, pair):
        values = []
        for z in pair:
            if t == 0:
                values.append(loaded(start, z))
            else:
                pad = pads.at[t]
                values.append(select(wall_of(z), opposite(pad[z + 3]), streamed(pad, z, 1)))
        v = side_by_side(values)
        v_hi = v.astype(BF16).astype(F32)
        x = jnp.concatenate([v_hi, v - v_hi, v_hi, ones], axis=0).astype(BF16)
        for i, z in enumerate(pair):
            xs[t, :, cells_of(z)] = x[:, PLANE * i : PLANE * i + PLANE]
        halves = []
        for c in range(2):
            rows = slice(256 * c, 256 * c + 256)
            act = jnp.dot(w_stack[rows, :], x, preferred_element_type=F32)
            wide = jnp.tanh(act)
            h = wide.astype(BF16)
            for i, z in enumerate(pair):
                hid[t, rows, cells_of(z)] = h[:, PLANE * i : PLANE * i + PLANE]
            if t == 2:
                wide = h.astype(F32)
                dh = side_by_side([dhs[rows, cells_of(z)] for z in pair]).astype(F32)
                h = (dh * (1.0 - wide * wide)).astype(BF16)
                for i, z in enumerate(pair):
                    dact[rows, cells_of(z)] = h[:, PLANE * i : PLANE * i + PLANE]
            halves.append(h)
        return v, jnp.concatenate(halves, axis=0)

    def forward_change(t, pair, done):
        if t == 2:
            g = side_by_side([state[z] for z in pair])
            backward_change(2, pair, (g, done[1]))
        else:
            v, h = done
            change = jnp.dot(wo_trans[...], h, preferred_element_type=F32)
            for i, z in enumerate(pair):
                cut = slice(PLANE * i, PLANE * i + PLANE)
                pads[t + 1, z + 3] = v[:, cut] + change[:, cut] + bias[...]

    def outgoing(z, g, slot):
        wall = wall_of(z)
        nothing = jnp.zeros((ROWS, PLANE), F32)
        bounce[z] = select(wall, opposite(g), nothing)
        pads[slot, z + 3] = select(wall, nothing, g)

    def backward_post(t, pair):
        slot = (4, 3, 0)[t]
        posts = [streamed(pads.at[slot], z, -1) + bounce[z] for z in pair]
        acc_b[...] += posts[0] + posts[1]
        g_post = side_by_side(posts)
        gb = jnp.concatenate([g_post, jnp.zeros((8, 2 * PLANE), F32)], axis=0).astype(BF16)
        for i, z in enumerate(pair):
            gbs[:, cells_of(z)] = gb[:, PLANE * i : PLANE * i + PLANE]
            if t != 1:
                state[z] = posts[i]
        return g_post, gb

    def backward_ahead(pair):
        g_post, gb = backward_post(2, pair)
        for c in range(2):
            rows = slice(256 * c, 256 * c + 256)
            dh = jnp.dot(wo[rows, :], gb, preferred_element_type=F32).astype(BF16)
            for i, z in enumerate(pair):
                dhs[rows, cells_of(z)] = dh[:, PLANE * i : PLANE * i + PLANE]

    def backward_hidden(t, pair):
        g_post, gb = backward_post(t, pair)
        halves = []
        for c in range(2):
            rows = slice(256 * c, 256 * c + 256)
            dh = jnp.dot(wo[rows, :], gb, preferred_element_type=F32)
            h = side_by_side([hid[t, rows, cells_of(z)] for z in pair]).astype(F32)
            da = (dh * (1.0 - h * h)).astype(BF16)
            for i, z in enumerate(pair):
                dact[rows, cells_of(z)] = da[:, PLANE * i : PLANE * i + PLANE]
            halves.append(da)
        return g_post, jnp.concatenate(halves, axis=0)

    def backward_field(pair):
        da = side_by_side([dact[:, cells_of(z)] for z in pair])
        change = jnp.dot(w_trans[...], da, preferred_element_type=F32)
        for i, z in enumerate(pair):
            g = state[z] + change[:, PLANE * i : PLANE * i + PLANE]
            for half in range(2):
                start[half, ROWS * z : ROWS * z + ROWS, :] = g[:, 128 * half : 128 * half + 128]

    def backward_change(t, pair, done):
        g_post, da = done
        g = g_post + jnp.dot(w_trans[...], da, preferred_element_type=F32)
        for i, z in enumerate(pair):
            cut = slice(PLANE * i, PLANE * i + PLANE)
            outgoing(z, g[:, cut], 5 - t)

    def grads(t):
        g_in = lax.dot_general(xs[t], dact[...], NT, preferred_element_type=F32)
        g_out = lax.dot_general(gbs[...], hid[t], NT, preferred_element_type=F32)
        if t == 2:
            acc_in[...] = g_in
            acc_out[...] = g_out
        else:
            acc_in[...] += g_in
            acc_out[...] += g_out

    def halo(slot, sign):
        first, second = (up, down) if sign == 1 else (down, up)
        pad = pads.at[slot]
        if sign == 1:
            moves = [
                (pad.at[10, 0:16], pad.at[2, 0:16], up),
                (pad.at[8:10, 0:8], pad.at[0:2, 0:8], up),
                (pad.at[3, 8:24], pad.at[11, 8:24], down),
                (pad.at[4:6, 16:24], pad.at[12:14, 16:24], down),
            ]
        else:
            moves = [
                (pad.at[3, 0:16], pad.at[11, 0:16], down),
                (pad.at[4:6, 0:8], pad.at[12:14, 0:8], down),
                (pad.at[10, 8:24], pad.at[2, 8:24], up),
                (pad.at[8:10, 16:24], pad.at[0:2, 16:24], up),
            ]
        return [
            pltpu.make_async_remote_copy(
                src_ref=src, dst_ref=dst, send_sem=halo_send.at[slot, i], recv_sem=halo_recv.at[slot, i],
                device_id=to, device_id_type=MESH,
            )
            for i, (src, dst, to) in enumerate(moves)
        ]

    def begin(copies):
        for copy in copies:
            copy.start()

    def end(copies):
        for copy in copies:
            copy.wait_recv()

    MIDDLE, OUTER = [(3, 4)], [(0, 1), (2, 5), (6, 7)]

    def in_turn(first, second, t, pairs, before=None):
        done = None
        for pair in pairs:
            if before is not None and pair in OUTER:
                end(before)
                before = None
            now = first(t, pair)
            if done is not None:
                second(t, *done)
            done = (pair, now)
        second(t, *done)

    def forwards(t, pairs, before=None):
        in_turn(forward_hidden, forward_change, t, pairs, before)

    def nothing(t, pair, done):
        pass

    forwards(0, OUTER)
    for copy in copies_in[6:8]:
        copy.wait()
    pl.semaphore_wait(barrier, len(peers))
    copy_1 = halo(1, 1)
    begin(copy_1)
    thick_t = floats[184:224, 0:64].astype(BF16)
    w_trans[...] = jnp.dot(thick_t, stack.astype(BF16), preferred_element_type=F32).astype(BF16)
    wo[...] = by_row.T.astype(BF16)
    for z in range(CZ):
        walls[z] = jnp.broadcast_to(solid[0, z : z + 1, :], (8, PLANE))
    copies_in[8].wait()
    by_plane(cotangent, back_in)
    for z in range(CZ):
        outgoing(z, loaded(back_in, z), 0)
    acc_b[...] = jnp.zeros((ROWS, PLANE), F32)
    copy_0 = halo(0, -1)
    begin(copy_0)
    forwards(0, MIDDLE)
    forwards(1, MIDDLE + OUTER, copy_1)
    copy_2 = halo(2, 1)
    begin(copy_2)
    end(copy_0)
    for pair in MIDDLE + OUTER:
        backward_ahead(pair)
    end(copy_2)
    forwards(2, OUTER)
    copy_3 = halo(3, -1)
    begin(copy_3)
    forwards(2, MIDDLE)
    grads(2)
    in_turn(backward_hidden, backward_change, 1, MIDDLE + OUTER, copy_3)
    copy_4 = halo(4, -1)
    begin(copy_4)
    grads(1)
    in_turn(backward_hidden, nothing, 0, MIDDLE + OUTER, copy_4)
    grads(0)

    def two(v):
        v_hi = v.astype(BF16).astype(F32)
        return v_hi, v - v_hi

    a_hi, a_low = two(acc_in[...])
    f_hi, f_low = two(floats[64:88, :])
    left = jnp.concatenate([f_hi, f_hi], axis=1).astype(BF16)
    right = jnp.concatenate([a_hi, a_low], axis=0).astype(BF16)
    upper = jnp.dot(left, right, preferred_element_type=F32)
    upper = upper + jnp.dot(f_low.astype(BF16), a_hi.astype(BF16), preferred_element_type=F32)
    b_hi, b_low = two(acc_b[...])
    pair = jnp.concatenate([b_hi, jnp.zeros((24, PLANE), F32), b_low, jnp.zeros((24, PLANE), F32)], axis=0).astype(BF16)
    line = lax.dot_general(jnp.ones((8, PLANE), BF16), pair, NT, preferred_element_type=F32)
    line = line + jnp.concatenate([line[:, 64:], line[:, :64]], axis=1)
    line = jnp.take_along_axis(line, ints[4, 0:8], axis=1, mode="promise_in_bounds")
    parts[MOM + 1 : 24] = jnp.zeros((23 - MOM, 4, 128), F32)
    for j in range(4):
        cut = slice(128 * j, 128 * j + 128)
        for row in range(MOM + 1):
            parts[row, j : j + 1, :] = upper[row : row + 1, cut]
        for row in range(Q):
            parts[24 + WHERE[row], j : j + 1, :] = acc_out[row : row + 1, cut]
        parts[63, j : j + 1, :] = line[0:1] if j == 0 else jnp.zeros((1, 128), F32)

    def remote(src, dst, send, recv, to):
        return pltpu.make_async_remote_copy(
            src_ref=src, dst_ref=dst, send_sem=send, recv_sem=recv, device_id=to, device_id_type=MESH
        )

    mine = core * 32
    other = 32 - mine
    swap = remote(parts.at[pl.ds(other, 32)], from_core, core_send.at[0], core_recv.at[0], partner)
    swap.start()

    for pair in MIDDLE + OUTER:
        backward_field(pair)
    for half in range(2):
        for row in range(Q):
            by_q[0, WHERE[row], :, 128 * half : 128 * half + 128] = start[half, pl.ds(row, CZ, stride=ROWS), :]

    field_out = pltpu.make_async_copy(by_q, d_field, out_sem.at[0])
    field_out.start()
    swap.wait_recv()
    merged[...] = parts[pl.ds(mine, 32)] + from_core[...]
    per = 32 // (ny * nx)
    share = lambda dy, dx: (lax.rem(me_y + dy, ny) * nx + lax.rem(me_x + dx, nx)) * per
    scatter = []
    for i, (dy, dx) in enumerate(others):
        src = merged.at[pl.ds(share(dy, dx), per)]
        scatter.append(remote(src, from_xy.at[i], xy_send.at[i], xy_recv.at[i], at(dy, dx)))
    begin(scatter)
    end(scatter)
    total = merged[pl.ds(share(0, 0), per)]
    for i in range(len(others)):
        total = total + from_xy[i]

    from_z[me_z] = total
    far_first = sorted(range(1, nz), key=lambda k: -min(k, nz - k))
    along = [
        remote(from_z.at[me_z], from_z.at[me_z], z_send.at[k - 1], z_recv.at[k - 1], at_z(k)) for k in far_first
    ]
    begin(along)
    end(along)
    total = from_z[0]
    for k in range(1, nz):
        total = total + from_z[k]

    own = pl.ds(mine + share(0, 0), per)
    final[own] = total * scale
    spread_out = [
        remote(final.at[own], final.at[own], e_send.at[i], e_recv.at[i], at(dy, dx)) for i, (dy, dx) in enumerate(others)
    ]
    begin(spread_out)
    give = []
    for k in sorted(range(ny), key=lambda k: hops(k, ny)):
        for i, (dy, dx) in enumerate(others):
            if dy == k:
                spread_out[i].wait_recv()
        line_of_x = final.at[pl.ds(mine + lax.rem(me_y + ny - k, ny) * nx * per, nx * per)]
        give.append(remote(line_of_x, line_of_x, g_send.at[k], g_recv.at[k], partner))
        give[-1].start()
    end(give)
    sums_out = pltpu.make_async_copy(final, sums, out_sem.at[1])
    sums_out.start()
    for copies in (copy_0, copy_1, copy_2, copy_3, copy_4, [swap], scatter, along, spread_out, give):
        for copy in copies:
            copy.wait_send()
    field_out.wait()
    sums_out.wait()


def write_out(field_at, sums_at, d_field, g_w_in, g_b_in, g_w_out, g_b_out, field, sums, a, b, c, d, sem):
    field_in = pltpu.make_async_copy(field_at, field, sem.at[0])
    sums_in = pltpu.make_async_copy(sums_at, sums, sem.at[1])
    sums_in.start()
    field_in.start()
    sums_in.wait()
    for j in range(4):
        cut = slice(128 * j, 128 * j + 128)
        for row in range(MOM):
            a[row : row + 1, cut] = sums[row, j : j + 1, :]
        b[:, cut] = sums[MOM, j : j + 1, :]
        for row in range(Q):
            c[row : row + 1, cut] = sums[24 + row, j : j + 1, :]
    d[...] = sums[63, 0:1, 0:Q]
    small = [
        pltpu.make_async_copy(src, dst, sem.at[i])
        for i, (src, dst) in enumerate([(a, g_w_in), (b, g_b_in), (c, g_w_out), (d, g_b_out)], 2)
    ]
    for copy in small:
        copy.start()
    field_in.wait()
    big = pltpu.make_async_copy(field, d_field, sem.at[6])
    big.start()
    for copy in small + [big]:
        copy.wait()


def solution(mesh):
    n_space, nx = mesh.shape["space"], mesh.shape["traj"]
    ny = 8 if n_space % 16 == 0 else 2
    nz = n_space // (2 * ny)
    scale = 1.0 / math.sqrt(float(n_space * nx * CELLS * STEPS))
    per = 32 // (ny * nx)
    hbm = pl.BlockSpec(memory_space=pltpu.HBM)
    dma = pltpu.SemaphoreType.DMA

    def per_device(field, solid, cotangent, w_in, b_in, w_out, b_out):
        def body(*refs):
            kernel((ny, nz, nx), scale, *refs)

        d_field, sums = pl.pallas_call(
            body,
            out_shape=(jax.ShapeDtypeStruct(field.shape, F32), jax.ShapeDtypeStruct((64, 4, 128), F32)),
            in_specs=[hbm] * 9,
            out_specs=(hbm, hbm),
            scratch_shapes=[
                pltpu.VMEM(field.shape, F32),
                pltpu.VMEM(solid.shape, jnp.int32),
                pltpu.VMEM(field.shape, F32),
                pltpu.VMEM(w_in.shape, BF16),
                pltpu.VMEM((1, HID), F32),
                pltpu.VMEM((Q, HID), BF16),
                pltpu.VMEM((1, Q), F32),
                pltpu.VMEM(FLOATS.shape, F32),
                pltpu.VMEM(INTS.shape, jnp.int32),
                pltpu.VMEM(field.shape, F32),
                dma((9,)),
                dma((2,)),
                pltpu.VMEM((5, CZ + 6, ROWS, PLANE), F32),
                pltpu.VMEM((2, CZ * ROWS, 128), F32),
                pltpu.VMEM((2, CZ * ROWS, 128), F32),
                pltpu.VMEM((CZ, ROWS, PLANE), F32),
                pltpu.VMEM((CZ, ROWS, PLANE), F32),
                pltpu.VMEM((CZ, 8, PLANE), jnp.int32),
                pltpu.VMEM((STEPS, 128, CELLS), BF16),
                pltpu.VMEM((STEPS, HID, CELLS), BF16),
                pltpu.VMEM((HID, CELLS), BF16),
                pltpu.VMEM((HID, CELLS), BF16),
                pltpu.VMEM((48, CELLS), BF16),
                pltpu.VMEM((HID, 128), BF16),
                pltpu.VMEM((ROWS, HID), BF16),
                pltpu.VMEM((HID, 48), BF16),
                pltpu.VMEM((ROWS, HID), BF16),
                pltpu.VMEM((ROWS, PLANE), F32),
                pltpu.VMEM((128, HID), F32),
                pltpu.VMEM((48, HID), F32),
                pltpu.VMEM((ROWS, PLANE), F32),
                pltpu.VMEM((64, 4, 128), F32),
                pltpu.VMEM((32, 4, 128), F32),
                pltpu.VMEM((ny * nx - 1, per, 4, 128), F32),
                pltpu.VMEM((nz, per, 4, 128), F32),
                pltpu.VMEM((32, 4, 128), F32),
                pltpu.VMEM((64, 4, 128), F32),
                dma((5, 4)), dma((5, 4)), dma((2,)), dma((2,)), dma((ny * nx - 1,)), dma((ny * nx - 1,)),
                dma((nz - 1,)), dma((nz - 1,)), dma((ny * nx - 1,)), dma((ny * nx - 1,)), dma((ny,)), dma((ny,)),
            ],
            compiler_params=pltpu.CompilerParams(collective_id=0, has_side_effects=True, vmem_limit_bytes=62 << 20,
           ),
            name="adjoint",
        )(field, solid, cotangent, w_in, b_in.reshape(1, HID), w_out.T, b_out.reshape(1, Q), jnp.asarray(FLOATS), jnp.asarray(INTS))
        d_field, g_w_in, g_b_in, g_w_out, g_b_out = pl.pallas_call(
            write_out,
            out_shape=(
                jax.ShapeDtypeStruct(field.shape, F32),
                jax.ShapeDtypeStruct((MOM, HID), F32),
                jax.ShapeDtypeStruct((1, HID), F32),
                jax.ShapeDtypeStruct((Q, HID), F32),
                jax.ShapeDtypeStruct((1, Q), F32),
            ),
            in_specs=[hbm, hbm],
            out_specs=(hbm,) * 5,
            scratch_shapes=[
                pltpu.VMEM(field.shape, F32), pltpu.VMEM((64, 4, 128), F32),
                pltpu.VMEM((MOM, HID), F32), pltpu.VMEM((1, HID), F32), pltpu.VMEM((Q, HID), F32), pltpu.VMEM((1, Q), F32),
                dma((7,)),
            ],
            compiler_params=pltpu.CompilerParams(vmem_limit_bytes=62 << 20),
            name="write_out",
        )(d_field, sums)
        return d_field, g_w_in, g_b_in.reshape(HID), g_w_out.T, g_b_out.reshape(Q)

    return jax.shard_map(
        per_device,
        mesh=mesh,
        in_specs=(P("traj", None, "space", None), P("traj", "space", None), P("traj", None, "space", None), P(), P(), P(), P()),
        out_specs=(P("traj", None, "space", None), P(), P(), P(), P()),
        check_vma=False,
    )
```
